32 devices in a mesh: gx: 8 (over z, x), gy: 4 (over y, core).
Axes of the slice: x: 2, y: 2, z: 4, core: 2. Of those that a mesh axis runs over, the one named last changes fastest.
Arguments:
- increment: bfloat16 [64, 384, 512], P(None, 'gx', 'gy'), may hold values from -6 to 6
- ensemble: bfloat16 [4, 64, 384, 512], P(None, None, 'gx', 'gy'), may hold values from -6 to 6
- wind_u: bfloat16 [64, 384, 512], P(None, 'gx', 'gy'), may hold values from -0.94921875 to 0.94921875
- wind_v: bfloat16 [64, 384, 512], P(None, 'gx', 'gy'), may hold values from -0.94921875 to 0.94921875
- filter_length: float32 [64], replicated, may hold values from 8 to 3072
- jacobian: bfloat16 [32, 512, 64], P(('gx', 'gy')), may hold values from -0.75 to 0.75
- obs_weight: float32 [32, 512], P(('gx', 'gy')), may hold values from 0.1 to 1
- departure: bfloat16 [2048, 512, 128], P(('gx', 'gy')), may hold values from -6 to 6
- obs_home: int32 [2048], P(('gx', 'gy')), may hold values from 0 to 31, as said below
- obs_line: int32 [2048], P(('gx', 'gy')), may hold values from 0 to 47
- obs_count: int32 [2048], P(('gx', 'gy')), may hold values from 1 to 128
Outputs:
- grad_alpha: float32 [4, 64, 384, 512], P(None, None, 'gx', 'gy')
- grad_static: float32 [64, 384, 512], P(None, 'gx', 'gy')
The draws below stay inside these ranges and needn't reach their ends.
Inputs may be any that keep to these rules, and one draw needn't show every extreme that they name: `obs_home`: the records of one device name 32 distinct grid devices, each exactly 2 times.
All inputs are finite; a program needn't handle non-finite values.
Results may differ from the reference program's by a relative error of at most 0.003.
Values may be sent and summed in bfloat16 or wider, within the bound.
A program may use at most 192 MiB of HBM per device.

```python
import math
import jax
import jax.numpy as jnp
from jax import lax

CX = 48
CY = 128
LEV = 64
CH = 512
MEM = 4
OBS_DEV = 64
HOMES = 32
MOST = 2
NX = 384
NY = 512
RECORDS = 2048
N_GX = 8
N_GY = 4


def draw_obs_home(key, part):
    subkeys = jax.random.split(jax.random.fold_in(key, 17), 3)
    levels = jax.random.randint(subkeys[0], (HOMES,), 0, 4)
    weights = 1 + 3 * levels
    scores = jax.random.randint(subkeys[1], (HOMES, HOMES), 0, 4096) * weights[None, :]
    scores = scores * HOMES + jnp.arange(HOMES)[None, :]
    picked = lax.top_k(scores, OBS_DEV // MOST)[1]
    repeated = jnp.repeat(picked, MOST, axis=1)
    shuffle = jax.random.randint(subkeys[2], (HOMES, OBS_DEV), 0, 4096) * OBS_DEV + jnp.arange(OBS_DEV)[None, :]
    ordering = jnp.argsort(shuffle, axis=1, stable=True)
    return jnp.take_along_axis(repeated, ordering, axis=1).reshape(HOMES * OBS_DEV).astype(jnp.int32)


def touch_ends(array, stream_key, smallest, largest):
    extent = array.shape
    index_at = [jax.random.randint(jax.random.fold_in(stream_key, axis), (), 0, extent[axis]) for axis in range(len(extent))]
    array = array.at[tuple(index_at)].set(smallest)
    longest = extent.index(max(extent))
    index_at[longest] = (index_at[longest] + 1) % extent[longest]
    return array.at[tuple(index_at)].set(largest)


def shard_levels(key, shape, pieces, low, top_value):
    def one(position, shards_of):
        heights = jax.random.uniform(jax.random.fold_in(jax.random.fold_in(key, 6), position), (shards_of,), jnp.float32, low / len(pieces), top_value / len(pieces))
        return jnp.repeat(jnp.exp(heights), shape[position] // shards_of).reshape((-1,) + (1,) * (len(shape) - position - 1))

    level = one(*pieces[0])
    for cut in pieces[1:]:
        level = level * one(*cut)
    return level


def bell_draw(rng, shape, scale, bound, shards=(), held_as=jnp.bfloat16):
    drawn = scale * jax.random.normal(rng, shape, jnp.float32)
    if shards:
        drawn = drawn * shard_levels(rng, shape, shards, -0.22, 0.18)
    return jnp.clip(drawn, -bound, bound).astype(held_as)


def setup_inputs(seed: int = 0) -> dict:
    key_of = jax.random.split(jax.random.key(seed), 12)
    increment = bell_draw(key_of[0], (LEV, NX, NY), 1.0, 6.0, ((1, 8), (2, 4)))
    ensemble = bell_draw(key_of[1], (MEM, LEV, NX, NY), 1.0, 6.0, ((2, 8), (3, 4)))
    wind_u = jnp.clip(jax.random.uniform(key_of[2], (LEV, NX, NY), jnp.float32, -0.94921875, 0.94921875) * shard_levels(key_of[2], (LEV, NX, NY), ((1, 8), (2, 4)), -0.4, 0.0), -0.94921875, 0.94921875).astype(jnp.bfloat16)
    wind_v = jnp.clip(jax.random.uniform(key_of[3], (LEV, NX, NY), jnp.float32, -0.94921875, 0.94921875) * shard_levels(key_of[3], (LEV, NX, NY), ((1, 8), (2, 4)), -0.4, 0.0), -0.94921875, 0.94921875).astype(jnp.bfloat16)
    filter_length = jnp.clip(jnp.exp(jax.random.uniform(key_of[4], (LEV,), jnp.float32, math.log(8.0), math.log(3072.0))), 8.0, 3072.0)
    jacobian = bell_draw(key_of[5], (HOMES, CH, LEV), LEV ** -0.5, 0.75, ((0, 32),))
    obs_weight = jnp.clip(jnp.exp(math.log(1.0) - 2.3025851 * jax.random.uniform(key_of[6], (HOMES, CH), jnp.float32) ** shard_levels(key_of[6], (HOMES, CH), ((0, 32),), -0.2, 0.2)), 0.1, 1.0)
    departure = bell_draw(key_of[7], (RECORDS, CH, CY), 1.0, 6.0, ((0, 32),))
    obs_home = draw_obs_home(jax.random.fold_in(key_of[11], 71), 0)
    obs_line = touch_ends(jax.random.randint(key_of[9], (RECORDS,), 0, CX), jax.random.fold_in(key_of[9], 1), 0, CX - 1).astype(jnp.int32)
    obs_count = touch_ends(jax.random.randint(key_of[10], (RECORDS,), 1, CY + 1), jax.random.fold_in(key_of[10], 1), 1, CY).astype(jnp.int32)
    return dict(increment=increment, ensemble=ensemble, wind_u=wind_u, wind_v=wind_v, filter_length=filter_length, jacobian=jacobian, obs_weight=obs_weight, departure=departure, obs_home=obs_home, obs_line=obs_line, obs_count=obs_count)


def recursive(field, coefs, decays, backward):

    def advance(state, column):
        updated = coefs[:, None] * column + decays[:, None] * state
        return (updated, updated)
    start = jnp.zeros(field.shape[1:], jnp.float32)
    _, result = lax.scan(advance, start, field, reverse=backward)
    return result

def smooth(field, forward_coef, backward_coef, decays):
    turned = jnp.transpose(field, (1, 0, 2))
    turned = recursive(turned, forward_coef, decays, False)
    turned = recursive(turned, backward_coef, decays, True)
    turned = jnp.transpose(turned, (2, 1, 0))
    turned = recursive(turned, forward_coef, decays, False)
    turned = recursive(turned, backward_coef, decays, True)
    return jnp.transpose(turned, (1, 2, 0))

def transport_x(static, speed):
    padded = jnp.pad(static, ((0, 0), (1, 1), (0, 0)))
    return static + jnp.maximum(speed, 0.0) * (padded[:, :-2, :] - static) + jnp.maximum(-speed, 0.0) * (padded[:, 2:, :] - static)

def transport_y(static, speed):
    padded = jnp.pad(static, ((0, 0), (0, 0), (1, 1)))
    return static + jnp.maximum(speed, 0.0) * (padded[:, :, :-2] - static) + jnp.maximum(-speed, 0.0) * (padded[:, :, 2:] - static)

def one_home(packed):
    matrix, weight_row, gathered, observed_dep, counts = packed
    matrix = matrix.astype(jnp.float32)
    predicted = jnp.einsum('cl,oly->ocy', matrix, gathered.astype(jnp.float32))
    observed = (jnp.arange(CY, dtype=jnp.int32)[None, :] < counts[:, None]).astype(jnp.float32)
    weighted = (weight_row[None, :, None] * (predicted - observed_dep.astype(jnp.float32)) * observed[:, None, :]).astype(jnp.bfloat16)
    adjoint = jnp.einsum('cl,ocy->oly', matrix, weighted.astype(jnp.float32))
    return adjoint.astype(jnp.bfloat16)

def reference(increment, ensemble, wind_u, wind_v, filter_length, jacobian, obs_weight, departure, obs_home, obs_line, obs_count):
    home_count = N_GX * N_GY
    grid_x = obs_home // N_GY * CX + obs_line
    grid_y = obs_home % N_GY
    block_id = (grid_x * N_GY + grid_y).astype(jnp.int32)
    blocks = jnp.transpose(increment.reshape(LEV, NX, N_GY, CY), (1, 2, 0, 3)).reshape(NX * N_GY, LEV, CY)
    gathered = blocks[block_id].reshape(home_count, OBS_DEV, LEV, CY)
    adjoints = lax.map(one_home, (jacobian, obs_weight, gathered, departure.reshape(home_count, OBS_DEV, CH, CY), obs_count.reshape(home_count, OBS_DEV)))
    summed = jnp.zeros((NX * N_GY, LEV, CY), jnp.float32).at[block_id].add(adjoints.reshape(home_count * OBS_DEV, LEV, CY).astype(jnp.float32))
    grad_obs = jnp.transpose(summed.reshape(NX, N_GY, LEV, CY), (2, 0, 1, 3)).reshape(LEV, NX, NY)
    decays = jnp.exp(-1.0 / filter_length)
    forward_coef = jnp.sqrt(-jnp.expm1(-2.0 / filter_length))
    backward_coef = -jnp.expm1(-1.0 / filter_length)
    grad_alpha = lax.map(lambda member: smooth(member.astype(jnp.float32) * grad_obs, forward_coef, backward_coef, decays), ensemble)
    static = smooth(grad_obs, forward_coef, backward_coef, decays)
    speed_x = wind_u.astype(jnp.float32)
    speed_y = wind_v.astype(jnp.float32)
    for sweep_index in range(3):
        static = transport_x(static, speed_x)
        static = transport_y(static, speed_y)
    return (grad_alpha, static)
```

```python
import functools
import jax
import jax.numpy as jnp
from jax import lax
from jax.experimental import pallas as pl
from jax.experimental.pallas import tpu as pltpu
from jax.sharding import PartitionSpec as P

HALO = 3
STRIP = 4
EDGE = 8
CODE = 32767.0
highest = lax.Precision.HIGHEST


def peer_id(axes, index):
    if len(axes) == 1:
        return {axes[0]: index}
    minor = lax.axis_size(axes[1])
    return {axes[0]: index // minor, axes[1]: index % minor}


def gather_kernel(axes, scatter, x_ref, o_ref, send_sem, recv_sem, own_sem):
    count = lax.axis_size(axes)
    me = lax.axis_index(axes[0])
    for name in axes[1:]:
        me = me * lax.axis_size(name) + lax.axis_index(name)
    barrier = pltpu.get_barrier_semaphore()

    def greet(k, _):
        pl.semaphore_signal(
            barrier,
            inc=1,
            device_id=peer_id(axes, lax.rem(me + k, count)),
            device_id_type=pl.DeviceIdType.MESH,
        )
        return 0

    lax.fori_loop(1, count, greet, 0)
    own = pltpu.make_async_copy(x_ref.at[me] if scatter else x_ref, o_ref.at[me], own_sem)
    own.start()
    pl.semaphore_wait(barrier, count - 1)

    def copy(k, slot):
        to = lax.rem(me + k, count)
        return pltpu.make_async_remote_copy(
            src_ref=x_ref.at[to] if scatter else x_ref,
            dst_ref=o_ref.at[slot],
            send_sem=send_sem.at[k],
            recv_sem=recv_sem.at[k],
            device_id=peer_id(axes, to),
            device_id_type=pl.DeviceIdType.MESH,
        )

    def send(k, _):
        copy(k, me).start()
        return 0

    def finish(k, _):
        landed = copy(k, lax.rem(me + count - k, count))
        landed.wait_send()
        landed.wait_recv()
        return 0

    lax.fori_loop(1, count, send, 0)
    own.wait()
    lax.fori_loop(1, count, finish, 0)


def exchange(x, axes, collective_id, scatter):
    count = lax.axis_size(axes)
    shape = x.shape if scatter else (count,) + x.shape
    return pl.pallas_call(
        functools.partial(gather_kernel, axes, scatter),
        out_shape=jax.ShapeDtypeStruct(shape, x.dtype),
        in_specs=[pl.BlockSpec(memory_space=pltpu.VMEM)],
        out_specs=pl.BlockSpec(memory_space=pltpu.VMEM),
        scratch_shapes=[
            pltpu.SemaphoreType.DMA((count,)),
            pltpu.SemaphoreType.DMA((count,)),
            pltpu.SemaphoreType.DMA,
        ],
        compiler_params=pltpu.CompilerParams(
            collective_id=collective_id, has_side_effects=True
        ),
        name="exchange_%d" % collective_id,
    )(x)


def split(value):
    high = value.astype(jnp.bfloat16)
    return high, (value - high.astype(jnp.float32)).astype(jnp.bfloat16)


def position(axes):
    me = lax.axis_index(axes[0])
    for name in axes[1:]:
        me = me * lax.axis_size(name) + lax.axis_index(name)
    return me


def coded(value):
    top = jnp.max(jnp.max(jnp.abs(value), axis=1, keepdims=True), axis=0, keepdims=True)
    top = jnp.maximum(top, 1e-30)
    code = jnp.round(value * (CODE / top)).astype(jnp.int32).astype(jnp.int16)
    return code, top * (1.0 / CODE)


def obs_kernel(
    axes, most, order_ref, line_ref, count_ref, j_ref, w_ref, d_hbm, got_ref, note_ref,
    d_buf, send_buf, note_buf, lhs_ref, hold_ref, scale_ref,
    d_sem, send_sem, recv_sem, note_send, note_recv,
):
    count = lax.axis_size(axes)
    half = count // 2
    me = position(axes)
    lev = j_ref.shape[1]
    cy = d_buf.shape[2]
    barrier = pltpu.get_barrier_semaphore()
    pieces = d_sem.shape[0]
    size = d_buf.shape[0] // pieces

    def piece(i):
        rows = pl.ds(i * size, size)
        return pltpu.make_async_copy(d_hbm.at[rows], d_buf.at[rows], d_sem.at[i])

    for i in range(pieces):
        piece(i).start()

    def greet(k, _):
        pl.semaphore_signal(
            barrier,
            inc=1,
            device_id=peer_id(axes, lax.rem(me + k, count)),
            device_id_type=pl.DeviceIdType.MESH,
        )
        return 0

    lax.fori_loop(1, count, greet, 0)
    turned = j_ref[...].astype(jnp.float32).T
    high, low = split(turned * w_ref[...])
    lhs_ref[...] = jnp.concatenate([high, low], axis=0)
    both = jnp.dot(lhs_ref[...], j_ref[...], preferred_element_type=jnp.float32)
    normal = both[:lev] + both[lev:]
    code, scale = coded(normal)
    hold_ref[...] = jnp.concatenate([code[: lev // 2], code[lev // 2 :]], axis=1)
    scale_ref[...] = jnp.broadcast_to(scale, scale_ref.shape)
    for i in range(pieces):
        piece(i).wait()
    pl.semaphore_wait(barrier, count - 1)
    lane = lax.broadcasted_iota(jnp.int32, (1, cy), 1)

    def fill(home, target, note):
        blocks = [d_buf[order_ref[home * most + m]] for m in range(most)]
        both = jnp.dot(
            lhs_ref[...], jnp.concatenate(blocks, axis=1), preferred_element_type=jnp.float32
        )
        word = jnp.where(lane == 3 * most, scale_ref[0:1, :], 0.0)
        for m in range(most):
            part = both[:lev, m * cy : (m + 1) * cy] + both[lev:, m * cy : (m + 1) * cy]
            code, scale = coded(part)
            target[m * lev : (m + 1) * lev, :] = code
            word = jnp.where(lane == m, line_ref[home * most + m].astype(jnp.float32), word)
            word = jnp.where(lane == most + m, count_ref[home * most + m].astype(jnp.float32), word)
            word = jnp.where(lane == 2 * most + m, scale, word)
        target[most * lev :, :] = hold_ref[...]
        note[...] = word

    def goal(t):
        j = t + t // half
        mine, place = me // half, lax.rem(me, half)
        other = lax.rem(mine + 1 + j // half, 2)
        return other * half + lax.rem(place + j, half)

    def sends(to, origin):
        peer = dict(device_id=peer_id(axes, to), device_id_type=pl.DeviceIdType.MESH)
        return (
            pltpu.make_async_remote_copy(
                src_ref=send_buf.at[to], dst_ref=got_ref.at[origin],
                send_sem=send_sem.at[to], recv_sem=recv_sem.at[origin], **peer
            ),
            pltpu.make_async_remote_copy(
                src_ref=note_buf.at[to], dst_ref=note_ref.at[origin],
                send_sem=note_send.at[to], recv_sem=note_recv.at[origin], **peer
            ),
        )

    def begin(to):
        for copy in sends(to, me):
            copy.start()

    first = goal(0)
    fill(first, send_buf.at[first], note_buf.at[first])

    def step(t, _):
        to = goal(t)
        fill(to, send_buf.at[to], note_buf.at[to])
        begin(goal(t - 1))
        return 0

    lax.fori_loop(1, count - 1, step, 0)
    fill(me, got_ref.at[me], note_ref.at[me])
    begin(goal(count - 2))

    def finish(k, _):
        peer = lax.rem(me + k, count)
        for copy in sends(peer, peer):
            copy.wait_send()
            copy.wait_recv()
        return 0

    lax.fori_loop(1, count, finish, 0)


def observe(order, lines, counts, jacobian, weight, departure, axes, most, collective_id):
    count = lax.axis_size(axes)
    channels, lev = jacobian.shape
    records, _, cy = departure.shape
    rows = most * lev + lev // 2
    smem = pl.BlockSpec(memory_space=pltpu.SMEM)
    vmem = pl.BlockSpec(memory_space=pltpu.VMEM)
    dma = pltpu.SemaphoreType.DMA
    return pl.pallas_call(
        functools.partial(obs_kernel, axes, most),
        out_shape=[
            jax.ShapeDtypeStruct((count, rows, cy), jnp.int16),
            jax.ShapeDtypeStruct((count, 1, cy), jnp.float32),
        ],
        in_specs=[smem, smem, smem, vmem, vmem, pl.BlockSpec(memory_space=pl.ANY)],
        out_specs=[vmem, vmem],
        scratch_shapes=[
            pltpu.VMEM((records, channels, cy), jnp.bfloat16),
            pltpu.VMEM((count, rows, cy), jnp.int16),
            pltpu.VMEM((count, 1, cy), jnp.float32),
            pltpu.VMEM((2 * lev, channels), jnp.bfloat16),
            pltpu.VMEM((lev // 2, 2 * lev), jnp.int16),
            pltpu.VMEM((8, cy), jnp.float32),
            dma((8,)), dma((count,)), dma((count,)), dma((count,)), dma((count,)),
        ],
        compiler_params=pltpu.CompilerParams(
            collective_id=collective_id,
            has_side_effects=True,
            vmem_limit_bytes=56 * 1024 * 1024,
        ),
        name="observe",
    )(order, lines, counts, jacobian, weight, departure)


def home_sums(most, note_ref, got_ref, c_ref, sum_ref):
    homes = got_ref.shape[0]
    lev, cy = c_ref.shape[1:]
    sum_ref[...] = jnp.zeros(sum_ref.shape, sum_ref.dtype)
    lane = lax.broadcasted_iota(jnp.int32, (lev // 2, 2 * lev), 1)
    column = lax.broadcasted_iota(jnp.int32, (lev, cy), 1)

    def one(k, _):
        code = got_ref[k, most * lev :, :].astype(jnp.int32).astype(jnp.float32)
        high, low = split(code)
        high, low = high.astype(jnp.float32), low.astype(jnp.float32)
        matrix = jnp.concatenate(
            [
                jnp.where(lane < lev, high, pltpu.roll(low, lev, 1)),
                jnp.where(lane < lev, pltpu.roll(high, lev, 1), low),
            ],
            axis=0,
        ).astype(jnp.bfloat16)
        lines = [note_ref[k, 0, m].astype(jnp.int32) for m in range(most)]
        block = jnp.concatenate([c_ref[line] for line in lines], axis=1)
        product = jnp.dot(
            matrix, jnp.concatenate([block, block], axis=0), preferred_element_type=jnp.float32
        )
        for m in range(most):
            part = got_ref[k, m * lev : (m + 1) * lev, :].astype(jnp.int32).astype(jnp.float32)
            value = (
                note_ref[k, 0, 3 * most] * product[:, m * cy : (m + 1) * cy]
                - note_ref[k, 0, 2 * most + m] * part
            )
            value = jnp.where(column < note_ref[k, 0, most + m].astype(jnp.int32), value, 0.0)
            rows = pl.ds(pl.multiple_of(lines[m] * lev, lev), lev)
            sum_ref[rows, :] += value
        return 0

    lax.fori_loop(0, homes, one, 0)


def ways():
    return [(dx, dy) for dx in (-1, 0, 1) for dy in (-1, 0, 1) if (dx, dy) != (0, 0)]


def halo_kernel(low_x, high_x, low_y, high_y, from_x, from_y, send_sem, recv_sem):
    gx, gy = lax.axis_index("gx"), lax.axis_index("gy")
    size_x, size_y = lax.axis_size("gx"), lax.axis_size("gy")
    barrier = pltpu.get_barrier_semaphore()

    def present(dx, dy):
        x, y = gx + dx, gy + dy
        return (x >= 0) & (x < size_x) & (y >= 0) & (y < size_y)

    def copy(k, dx, dy):
        if dy == 0:
            source = high_x if dx == 1 else low_x
            target = from_x.at[0 if dx == 1 else 1]
        else:
            source = high_y if dy == 1 else low_y
            target = from_y.at[1 - dx, 0 if dy == 1 else 1]
        return pltpu.make_async_remote_copy(
            src_ref=source,
            dst_ref=target,
            send_sem=send_sem.at[k],
            recv_sem=recv_sem.at[k],
            device_id={"gx": gx + dx, "gy": gy + dy},
            device_id_type=pl.DeviceIdType.MESH,
        )

    around = 0
    for dx, dy in ways():
        around = around + present(dx, dy).astype(jnp.int32)

        @pl.when(present(dx, dy))
        def _():
            pl.semaphore_signal(
                barrier,
                inc=1,
                device_id={"gx": gx + dx, "gy": gy + dy},
                device_id_type=pl.DeviceIdType.MESH,
            )

    pl.semaphore_wait(barrier, around)
    for k, (dx, dy) in enumerate(ways()):

        @pl.when(present(dx, dy))
        def _():
            copy(k, dx, dy).start()

    for k, (dx, dy) in enumerate(ways()):

        @pl.when(jnp.logical_not(present(-dx, -dy)))
        def _():
            if dy == 0:
                slot = 0 if dx == 1 else 1
                from_x[slot] = jnp.zeros(from_x.shape[1:], from_x.dtype)
            else:
                slot = 0 if dy == 1 else 1
                from_y[1 - dx, slot] = jnp.zeros(from_y.shape[2:], from_y.dtype)

    for k, (dx, dy) in enumerate(ways()):

        @pl.when(present(dx, dy))
        def _():
            copy(k, dx, dy).wait_send()

        @pl.when(present(-dx, -dy))
        def _():
            copy(k, dx, dy).wait_recv()


def halo(low_x, high_x, low_y, high_y, collective_id):
    return pl.pallas_call(
        halo_kernel,
        out_shape=[
            jax.ShapeDtypeStruct((2,) + low_x.shape, low_x.dtype),
            jax.ShapeDtypeStruct((3, 2) + low_y.shape, low_y.dtype),
        ],
        in_specs=[pl.BlockSpec(memory_space=pltpu.VMEM)] * 4,
        out_specs=[pl.BlockSpec(memory_space=pltpu.VMEM)] * 2,
        scratch_shapes=[pltpu.SemaphoreType.DMA((8,)), pltpu.SemaphoreType.DMA((8,))],
        compiler_params=pltpu.CompilerParams(
            collective_id=collective_id, has_side_effects=True
        ),
        name="halo",
    )(low_x, high_x, low_y, high_y)


def edge_columns(cy, width):
    row = lax.broadcasted_iota(jnp.int32, (2 * width, cy), 0)
    col = lax.broadcasted_iota(jnp.int32, (2 * width, cy), 1)
    return (col == jnp.where(row < width, row, row + cy - 2 * width)).astype(jnp.bfloat16)


def local_kernel(
    members, most, note_ref, got_ref, c_ref, e_ref, mx_ref, wy_ref,
    x_ref, sx_ref, sy_ref, rows_ref, sum_ref,
):
    _, levels, cx, cy = e_ref.shape
    lev = c_ref.shape[1]

    @pl.when(pl.program_id(0) == 0)
    def _():
        home_sums(most, note_ref, got_ref, c_ref, sum_ref)

    for l in range(levels):
        base = sum_ref[pl.ds(pl.program_id(0) * levels + l, cx, stride=lev), :]
        parts = [base] + [e_ref[m, l].astype(jnp.float32) * base for m in range(members)]
        high, low = split(jnp.concatenate(parts, axis=1))
        result = jnp.dot(
            mx_ref[l],
            jnp.concatenate([high, high, low], axis=0),
            preferred_element_type=jnp.float32,
        )
        stack = jnp.concatenate(
            [result[:cx, m * cy : (m + 1) * cy] for m in range(members + 1)], axis=0
        )
        x_ref[l] = stack
        for m in range(members + 1):
            rows_ref[m, l : l + 1, :] = result[cx : cx + 1, m * cy : (m + 1) * cy]
            rows_ref[members + 1 + m, l : l + 1, :] = result[0:1, m * cy : (m + 1) * cy]
        high, low = split(stack)
        sums = lax.dot_general(
            wy_ref[l],
            jnp.concatenate([high, low], axis=1),
            (((1,), (1,)), ((), ())),
            preferred_element_type=jnp.float32,
        )
        sy_ref[l] = sums[0:8] + sums[8:16]
    sx_ref[...] = rows_ref[...].astype(sx_ref.dtype)


def final_kernel(
    members, x_ref, ux_ref, ex_ref, my_ref, uy_ref, ey_ref, u_ref, v_ref,
    a_ref, s_ref, low_x, high_x, low_y, high_y,
):
    levels = x_ref.shape[0]
    _, _, cx, cy = a_ref.shape
    first = (((0,), (0,)), ((), ()))
    columns = edge_columns(cy, STRIP)
    for l in range(levels):
        field = x_ref[l] + lax.dot_general(
            ux_ref[l], ex_ref[l], first, preferred_element_type=jnp.float32
        )
        high, low = split(field)
        m_high, m_low = split(my_ref[l])
        weights = jnp.concatenate(
            [
                jnp.concatenate([m_high, m_low], axis=1),
                jnp.concatenate([m_high, jnp.zeros_like(m_low)], axis=1),
            ],
            axis=0,
        )
        both = jnp.dot(
            jnp.concatenate([high, low], axis=1), weights, preferred_element_type=jnp.float32
        )
        field = (
            both[:, :cy]
            + both[:, cy:]
            + lax.dot_general(ey_ref[l], uy_ref[l], first, preferred_element_type=jnp.float32)
        )
        static = field[:cx]
        s_ref[l] = static
        for m in range(members):
            a_ref[m, l] = field[(m + 1) * cx : (m + 2) * cx]
        for k, value in enumerate((static.astype(jnp.bfloat16), u_ref[l], v_ref[l])):
            low_x[k, l] = value[:STRIP]
            high_x[k, l] = value[cx - STRIP :]
            sides = lax.dot_general(
                columns, value, (((1,), (1,)), ((), ())), preferred_element_type=jnp.float32
            )
            low_y[k, l] = sides[:STRIP].astype(low_y.dtype)
            high_y[k, l] = sides[STRIP:].astype(high_y.dtype)


def transport_kernel(s_ref, u_ref, v_ref, hx_ref, hy_ref, o_ref):
    levels, cx, cy = o_ref.shape
    rows, lanes = cx + 2 * EDGE, 2 * cy
    blank = jnp.zeros((EDGE - STRIP, cy), jnp.float32)
    place = edge_columns(cy, STRIP)

    def widened(value, k, l):
        strips = []
        for j in range(3):
            pair = jnp.concatenate(
                [
                    hy_ref[j, 1, k, l].astype(jnp.float32),
                    hy_ref[j, 0, k, l].astype(jnp.float32),
                ],
                axis=0,
            ).astype(jnp.bfloat16)
            strips.append(
                lax.dot_general(
                    pair, place, (((0,), (0,)), ((), ())), preferred_element_type=jnp.float32
                )
            )
        above = hx_ref[0, k, l].astype(jnp.float32)
        below = hx_ref[1, k, l].astype(jnp.float32)
        return jnp.concatenate(
            [
                jnp.concatenate([blank, above, value, below, blank], axis=0),
                jnp.concatenate([strips[0][cx - EDGE :], strips[1], strips[2][:EDGE]], axis=0),
            ],
            axis=1,
        )

    for l in range(levels):
        s = widened(s_ref[l], 0, l)
        u = widened(u_ref[l].astype(jnp.float32), 1, l)
        v = widened(v_ref[l].astype(jnp.float32), 2, l)
        east, north = u > 0.0, v > 0.0
        u, v = jnp.abs(u), jnp.abs(v)
        for _ in range(HALO):
            s = s + u * (jnp.where(east, pltpu.roll(s, 1, 0), pltpu.roll(s, rows - 1, 0)) - s)
            s = s + v * (jnp.where(north, pltpu.roll(s, 1, 1), pltpu.roll(s, lanes - 1, 1)) - s)
        o_ref[l] = s[EDGE : EDGE + cx, :cy]


def smoother(lengths, count):
    pos = jnp.arange(count, dtype=jnp.float32)
    far = jnp.abs(pos[:, None] - pos[None, :])
    left = count - jnp.maximum(pos[:, None], pos[None, :])
    lengths = lengths[:, None, None]
    scale = -jnp.expm1(-1.0 / lengths) / jnp.sqrt(-jnp.expm1(-2.0 / lengths))
    return scale * jnp.exp(-far[None] / lengths) * -jnp.expm1(-2.0 * left[None] / lengths)


def end_weights(lengths, count):
    pos = jnp.arange(count, dtype=jnp.float32)
    coef = jnp.sqrt(-jnp.expm1(-2.0 / lengths))
    return coef[:, None] * jnp.exp(-(count - 1.0 - pos)[None, :] / lengths[:, None])


def responses(lengths, count):
    pos = jnp.arange(count, dtype=jnp.float32)[None, :]
    lengths = lengths[:, None]
    coef = -jnp.expm1(-1.0 / lengths)
    ratio = jnp.expm1(-2.0 * (count - pos) / lengths) / jnp.expm1(-2.0 / lengths)
    ahead = coef * jnp.exp(-(pos + 1.0) / lengths) * ratio
    behind = jnp.exp(-(count - pos) / lengths)
    return ahead, behind


def combine_weights(lengths, count, size, me):
    link = responses(lengths, count)[0][:, 0]
    k = jnp.arange(size)

    def power(steps, ok):
        return jnp.where(
            ok[..., None],
            jnp.exp(-jnp.maximum(steps, 0)[..., None] * (count / lengths)),
            0.0,
        )

    ahead = power(me - 1 - k, k < me)
    behind = power(k - me - 1, k > me)
    pair = power(k[:, None] - 1 - k[None, :], k[None, :] < k[:, None])
    cross = link[None, :] * jnp.sum(behind[:, None, :] * pair, axis=0)
    return ahead, behind, cross


def two_parts(value):
    high = lax.reduce_precision(value, 8, 7)
    return high, value - high


def whole_tiles(parts):
    joined = jnp.concatenate(parts, axis=1)
    return jnp.pad(joined, ((0, 0), (0, -joined.shape[1] % 16), (0, 0))).astype(jnp.bfloat16)


def left_terms(value):
    high, low = two_parts(value)
    return whole_tiles([high, low, high])


def right_terms(value):
    high, low = two_parts(value)
    return whole_tiles([high, high, low])


def body(
    increment,
    ensemble,
    wind_u,
    wind_v,
    filter_length,
    jacobian,
    obs_weight,
    departure,
    obs_home,
    obs_line,
    obs_count,
):
    axes = ("gx", "gy")
    home_count = lax.axis_size(axes)
    records_here = obs_home.shape[0]
    most = (records_here + home_count - 1) // home_count
    lev, cx, cy = increment.shape
    members = ensemble.shape[0]
    fields = members + 1
    slot_count = home_count * most
    index = jnp.arange(records_here, dtype=jnp.int32)
    earlier = (obs_home[:, None] == obs_home[None, :]) & (index[None, :] < index[:, None])
    slot_of = obs_home * most + jnp.sum(earlier.astype(jnp.int32), axis=1)
    placing = slot_of[:, None] == jnp.arange(slot_count, dtype=jnp.int32)[None, :]
    order, lines, counts = [
        jnp.sum(jnp.where(placing, value[:, None], 0), axis=0)
        for value in (index, obs_line, obs_count)
    ]
    got, note = observe(
        order, lines, counts, jacobian[0], obs_weight, departure, axes, most, 3
    )
    smooth_x = smoother(filter_length, cx)
    rows_x = jnp.concatenate(
        [
            smooth_x,
            end_weights(filter_length, cx)[:, None, :],
            jnp.zeros((lev, EDGE - 1, cx), jnp.float32),
        ],
        axis=1,
    )
    high_x = lax.reduce_precision(rows_x, 8, 7)
    cat_x = jnp.concatenate([high_x, rows_x - high_x, high_x], axis=2).astype(jnp.bfloat16)
    smooth_y = smoother(filter_length, cy)
    sums_y = jnp.stack([end_weights(filter_length, cy), smooth_y[:, 0, :]], axis=1)
    high_y = lax.reduce_precision(sums_y, 8, 7)
    low_y = sums_y - high_y
    blank = jnp.zeros((lev, 6, 2 * cy), jnp.float32)
    cat_y = jnp.concatenate(
        [
            jnp.concatenate([high_y, high_y], axis=2),
            blank,
            jnp.concatenate([low_y, jnp.zeros_like(low_y)], axis=2),
            blank,
        ],
        axis=1,
    ).astype(jnp.bfloat16)

    out_x = jnp.stack(responses(filter_length, cx), axis=0)
    same = jnp.eye(fields, dtype=jnp.float32)
    block_x = left_terms(
        (
            jnp.moveaxis(out_x, 0, 1)[:, :, None, None, :] * same[None, None, :, :, None]
        ).reshape(lev, 2 * fields, fields * cx)
    )
    out_y = right_terms(jnp.stack(responses(filter_length, cy), axis=1))
    across = jnp.transpose(increment, (1, 0, 2))
    tile = 16
    steps = lev // tile
    def levels_first(*shape):
        return pl.BlockSpec((tile,) + shape, lambda i: (i, 0, 0))

    params = pltpu.CompilerParams(
        dimension_semantics=("arbitrary",), vmem_limit_bytes=56 * 1024 * 1024
    )
    local, state_x, state_y = pl.pallas_call(
        functools.partial(local_kernel, members, most),
        grid=(steps,),
        in_specs=[
            pl.BlockSpec(memory_space=pltpu.SMEM),
            pl.BlockSpec(got.shape, lambda i: (0, 0, 0), pipeline_mode=pl.Buffered(1)),
            pl.BlockSpec(across.shape, lambda i: (0, 0, 0), pipeline_mode=pl.Buffered(1)),
            pl.BlockSpec((members, tile, cx, cy), lambda i: (0, i, 0, 0)),
            levels_first(cx + EDGE, 3 * cx),
            levels_first(16, 2 * cy),
        ],
        out_specs=[
            levels_first(fields * cx, cy),
            pl.BlockSpec((2 * fields, tile, cy), lambda i: (0, i, 0)),
            levels_first(8, fields * cx),
        ],
        out_shape=[
            jax.ShapeDtypeStruct((lev, fields * cx, cy), jnp.float32),
            jax.ShapeDtypeStruct((2 * fields, lev, cy), jnp.bfloat16),
            jax.ShapeDtypeStruct((lev, 8, fields * cx), jnp.float32),
        ],
        scratch_shapes=[
            pltpu.VMEM((2 * fields, tile, cy), jnp.float32),
            pltpu.VMEM((cx * lev, cy), jnp.float32),
        ],
        compiler_params=params,
        name="local",
    )(note, got, across, ensemble, cat_x, cat_y)

    size_x = lax.axis_size("gx")
    part = lev // size_x
    own = lax.axis_index("gx") * part
    mine = lax.dynamic_slice_in_dim(filter_length, own, part, 0)
    sent = jnp.moveaxis(state_x.reshape(2 * fields, size_x, part, cy), 1, 0)
    all_x = exchange(sent, ("gx",), 1, True).astype(jnp.float32)
    ahead, behind, cross = [
        jnp.stack(w) for w in zip(*[combine_weights(mine, cx, size_x, d) for d in range(size_x)])
    ]
    front, back = all_x[:, :fields], all_x[:, fields:]
    enter_x = sum(ahead[:, k, None, :, None] * front[k][None] for k in range(size_x))
    leave_x = sum(
        behind[:, k, None, :, None] * back[k][None] + cross[:, k, None, :, None] * front[k][None]
        for k in range(size_x)
    )
    swept = jnp.concatenate([enter_x, leave_x], axis=1).astype(jnp.bfloat16)
    swept = exchange(swept, ("gx",), 4, True).astype(jnp.float32)
    swept = jnp.moveaxis(swept, 0, 1).reshape(2, fields, lev, cy)
    enter_x, leave_x = swept[0], swept[1]
    edges_x = jnp.stack([enter_x, leave_x], axis=0)
    extra = jnp.sum(
        edges_x[:, :, :, None, :] * jnp.moveaxis(sums_y, 1, 1)[None, None], axis=-1
    )
    state_y = jnp.moveaxis(state_y[:, :2], 1, 0).reshape(2, lev, fields, cx) + sum(
        jnp.moveaxis(extra[s], (0, 1, 2), (2, 1, 0))[..., None] * out_x[s][None, :, None, :]
        for s in range(2)
    )
    all_y = exchange(
        state_y.reshape(2, lev, fields * cx).astype(jnp.bfloat16), ("gy",), 2, False
    ).astype(jnp.float32)
    ahead, behind, cross = combine_weights(
        filter_length, cy, lax.axis_size("gy"), lax.axis_index("gy")
    )
    enter_y = jnp.sum(ahead[:, :, None] * all_y[:, 0], axis=0)
    leave_y = jnp.sum(
        behind[:, :, None] * all_y[:, 1] + cross[:, :, None] * all_y[:, 0], axis=0
    )
    edges_y = left_terms(jnp.stack([enter_y, leave_y], axis=1))
    edges_x = right_terms(jnp.moveaxis(edges_x.reshape(2 * fields, lev, cy), 0, 1))
    depth_x, depth_y = block_x.shape[1], edges_y.shape[1]
    grad_alpha, static, *strips = pl.pallas_call(
        functools.partial(final_kernel, members),
        grid=(steps,),
        in_specs=[
            levels_first(fields * cx, cy),
            levels_first(depth_x, fields * cx),
            levels_first(depth_x, cy),
            levels_first(cy, cy),
            levels_first(depth_y, cy),
            levels_first(depth_y, fields * cx),
            levels_first(cx, cy),
            levels_first(cx, cy),
        ],
        out_specs=[
            pl.BlockSpec((members, tile, cx, cy), lambda i: (0, i, 0, 0)),
            levels_first(cx, cy),
            pl.BlockSpec((3, tile, STRIP, cy), lambda i: (0, i, 0, 0)),
            pl.BlockSpec((3, tile, STRIP, cy), lambda i: (0, i, 0, 0)),
            pl.BlockSpec((3, tile, STRIP, cx), lambda i: (0, i, 0, 0)),
            pl.BlockSpec((3, tile, STRIP, cx), lambda i: (0, i, 0, 0)),
        ],
        out_shape=[
            jax.ShapeDtypeStruct((members, lev, cx, cy), jnp.float32),
            jax.ShapeDtypeStruct((lev, cx, cy), jnp.float32),
            jax.ShapeDtypeStruct((3, lev, STRIP, cy), jnp.bfloat16),
            jax.ShapeDtypeStruct((3, lev, STRIP, cy), jnp.bfloat16),
            jax.ShapeDtypeStruct((3, lev, STRIP, cx), jnp.bfloat16),
            jax.ShapeDtypeStruct((3, lev, STRIP, cx), jnp.bfloat16),
        ],
        compiler_params=params,
        name="final",
    )(local, block_x, edges_x, smooth_y, out_y, edges_y, wind_u, wind_v)

    halo_x, halo_y = halo(*strips, 5)
    static = pl.pallas_call(
        transport_kernel,
        grid=(steps,),
        in_specs=[
            levels_first(cx, cy),
            levels_first(cx, cy),
            levels_first(cx, cy),
            pl.BlockSpec((2, 3, tile, STRIP, cy), lambda i: (0, 0, i, 0, 0)),
            pl.BlockSpec((3, 2, 3, tile, STRIP, cx), lambda i: (0, 0, 0, i, 0, 0)),
        ],
        out_specs=levels_first(cx, cy),
        out_shape=jax.ShapeDtypeStruct((lev, cx, cy), jnp.float32),
        compiler_params=params,
        name="transport",
    )(static, wind_u, wind_v, halo_x, halo_y)
    return (grad_alpha, static)


def solution(mesh):
    return jax.shard_map(
        body,
        mesh=mesh,
        in_specs=(
            P(None, "gx", "gy"),
            P(None, None, "gx", "gy"),
            P(None, "gx", "gy"),
            P(None, "gx", "gy"),
            P(),
            P(("gx", "gy"), None, None),
            P(("gx", "gy"), None),
            P(("gx", "gy"), None, None),
            P(("gx", "gy")),
            P(("gx", "gy")),
            P(("gx", "gy")),
        ),
        out_specs=(P(None, None, "gx", "gy"), P(None, "gx", "gy")),
        check_vma=False,
    )
```

```python
import functools
import jax
import jax.numpy as jnp
from jax import lax
from jax.experimental import pallas as pl
from jax.experimental.pallas import tpu as pltpu
from jax.sharding import PartitionSpec as P

HALO = 3
STRIP = 4
EDGE = 8
CODE = 32767.0
highest = lax.Precision.HIGHEST


def peer_id(axes, index):
    if len(axes) == 1:
        return {axes[0]: index}
    minor = lax.axis_size(axes[1])
    return {axes[0]: index // minor, axes[1]: index % minor}


def split(value):
    high = value.astype(jnp.bfloat16)
    return high, (value - high.astype(jnp.float32)).astype(jnp.bfloat16)


def position(axes):
    me = lax.axis_index(axes[0])
    for name in axes[1:]:
        me = me * lax.axis_size(name) + lax.axis_index(name)
    return me


def coded(value):
    top = jnp.max(jnp.max(jnp.abs(value), axis=1, keepdims=True), axis=0, keepdims=True)
    top = jnp.maximum(top, 1e-30)
    code = jnp.round(value * (CODE / top)).astype(jnp.int32).astype(jnp.int16)
    return code, top * (1.0 / CODE)


def obs_kernel(
    axes, most, order_ref, line_ref, count_ref, j_ref, w_ref, d_hbm, got_ref, note_ref,
    d_buf, send_buf, note_buf, lhs_ref, hold_ref, scale_ref,
    d_sem, send_sem, recv_sem, note_send, note_recv,
):
    count = lax.axis_size(axes)
    half = count // 2
    me = position(axes)
    lev = j_ref.shape[1]
    cy = d_buf.shape[2]
    barrier = pltpu.get_barrier_semaphore()
    pieces = d_sem.shape[0]
    size = d_buf.shape[0] // pieces

    def piece(i):
        rows = pl.ds(i * size, size)
        return pltpu.make_async_copy(d_hbm.at[rows], d_buf.at[rows], d_sem.at[i])

    for i in range(pieces):
        piece(i).start()

    def greet(k, _):
        pl.semaphore_signal(
            barrier,
            inc=1,
            device_id=peer_id(axes, lax.rem(me + k, count)),
            device_id_type=pl.DeviceIdType.MESH,
        )
        return 0

    lax.fori_loop(1, count, greet, 0)
    turned = j_ref[...].astype(jnp.float32).T
    high, low = split(turned * w_ref[...])
    lhs_ref[...] = jnp.concatenate([high, low], axis=0)
    both = jnp.dot(lhs_ref[...], j_ref[...], preferred_element_type=jnp.float32)
    normal = both[:lev] + both[lev:]
    code, scale = coded(normal)
    hold_ref[...] = jnp.concatenate([code[: lev // 2], code[lev // 2 :]], axis=1)
    scale_ref[...] = jnp.broadcast_to(scale, scale_ref.shape)
    for i in range(pieces):
        piece(i).wait()
    pl.semaphore_wait(barrier, count - 1)
    lane = lax.broadcasted_iota(jnp.int32, (1, cy), 1)

    def fill(home, target, note):
        blocks = [d_buf[order_ref[home * most + m]] for m in range(most)]
        both = jnp.dot(
            lhs_ref[...], jnp.concatenate(blocks, axis=1), preferred_element_type=jnp.float32
        )
        word = jnp.where(lane == 3 * most, scale_ref[0:1, :], 0.0)
        for m in range(most):
            part = both[:lev, m * cy : (m + 1) * cy] + both[lev:, m * cy : (m + 1) * cy]
            code, scale = coded(part)
            target[m * lev : (m + 1) * lev, :] = code
            word = jnp.where(lane == m, line_ref[home * most + m].astype(jnp.float32), word)
            word = jnp.where(lane == most + m, count_ref[home * most + m].astype(jnp.float32), word)
            word = jnp.where(lane == 2 * most + m, scale, word)
        target[most * lev :, :] = hold_ref[...]
        note[...] = word

    def goal(t):
        j = t + t // half
        mine, place = me // half, lax.rem(me, half)
        other = lax.rem(mine + 1 + j // half, 2)
        return other * half + lax.rem(place + j, half)

    def sends(to, origin):
        peer = dict(device_id=peer_id(axes, to), device_id_type=pl.DeviceIdType.MESH)
        return (
            pltpu.make_async_remote_copy(
                src_ref=send_buf.at[to], dst_ref=got_ref.at[origin],
                send_sem=send_sem.at[to], recv_sem=recv_sem.at[origin], **peer
            ),
            pltpu.make_async_remote_copy(
                src_ref=note_buf.at[to], dst_ref=note_ref.at[origin],
                send_sem=note_send.at[to], recv_sem=note_recv.at[origin], **peer
            ),
        )

    def begin(to):
        for copy in sends(to, me):
            copy.start()

    first = goal(0)
    fill(first, send_buf.at[first], note_buf.at[first])

    def step(t, _):
        to = goal(t)
        fill(to, send_buf.at[to], note_buf.at[to])
        begin(goal(t - 1))
        return 0

    lax.fori_loop(1, count - 1, step, 0)
    fill(me, got_ref.at[me], note_ref.at[me])
    begin(goal(count - 2))

    def finish(k, _):
        peer = lax.rem(me + k, count)
        for copy in sends(peer, peer):
            copy.wait_send()
            copy.wait_recv()
        return 0

    lax.fori_loop(1, count, finish, 0)


def observe(order, lines, counts, jacobian, weight, departure, axes, most, collective_id):
    count = lax.axis_size(axes)
    channels, lev = jacobian.shape
    records, _, cy = departure.shape
    rows = most * lev + lev // 2
    smem = pl.BlockSpec(memory_space=pltpu.SMEM)
    vmem = pl.BlockSpec(memory_space=pltpu.VMEM)
    dma = pltpu.SemaphoreType.DMA
    return pl.pallas_call(
        functools.partial(obs_kernel, axes, most),
        out_shape=[
            jax.ShapeDtypeStruct((count, rows, cy), jnp.int16),
            jax.ShapeDtypeStruct((count, 1, cy), jnp.float32),
        ],
        in_specs=[smem, smem, smem, vmem, vmem, pl.BlockSpec(memory_space=pl.ANY)],
        out_specs=[vmem, vmem],
        scratch_shapes=[
            pltpu.VMEM((records, channels, cy), jnp.bfloat16),
            pltpu.VMEM((count, rows, cy), jnp.int16),
            pltpu.VMEM((count, 1, cy), jnp.float32),
            pltpu.VMEM((2 * lev, channels), jnp.bfloat16),
            pltpu.VMEM((lev // 2, 2 * lev), jnp.int16),
            pltpu.VMEM((8, cy), jnp.float32),
            dma((8,)), dma((count,)), dma((count,)), dma((count,)), dma((count,)),
        ],
        compiler_params=pltpu.CompilerParams(
            collective_id=collective_id,
            has_side_effects=True,
            vmem_limit_bytes=56 * 1024 * 1024,
        ),
        name="observe",
    )(order, lines, counts, jacobian, weight, departure)


def home_sums(most, note_ref, got_ref, c_ref, sum_ref):
    homes = got_ref.shape[0]
    lev, cy = c_ref.shape[1:]
    sum_ref[...] = jnp.zeros(sum_ref.shape, sum_ref.dtype)
    lane = lax.broadcasted_iota(jnp.int32, (lev // 2, 2 * lev), 1)
    column = lax.broadcasted_iota(jnp.int32, (lev, cy), 1)

    def one(k, _):
        code = got_ref[k, most * lev :, :].astype(jnp.int32).astype(jnp.float32)
        high, low = split(code)
        high, low = high.astype(jnp.float32), low.astype(jnp.float32)
        matrix = jnp.concatenate(
            [
                jnp.where(lane < lev, high, pltpu.roll(low, lev, 1)),
                jnp.where(lane < lev, pltpu.roll(high, lev, 1), low),
            ],
            axis=0,
        ).astype(jnp.bfloat16)
        lines = [note_ref[k, 0, m].astype(jnp.int32) for m in range(most)]
        block = jnp.concatenate([c_ref[line] for line in lines], axis=1)
        product = jnp.dot(
            matrix, jnp.concatenate([block, block], axis=0), preferred_element_type=jnp.float32
        )
        for m in range(most):
            part = got_ref[k, m * lev : (m + 1) * lev, :].astype(jnp.int32).astype(jnp.float32)
            value = (
                note_ref[k, 0, 3 * most] * product[:, m * cy : (m + 1) * cy]
                - note_ref[k, 0, 2 * most + m] * part
            )
            value = jnp.where(column < note_ref[k, 0, most + m].astype(jnp.int32), value, 0.0)
            rows = pl.ds(pl.multiple_of(lines[m] * lev, lev), lev)
            sum_ref[rows, :] += value
        return 0

    lax.fori_loop(0, homes, one, 0)


def ways():
    return [(dx, dy) for dx in (-1, 0, 1) for dy in (-1, 0, 1) if (dx, dy) != (0, 0)]


def halo_kernel(low_x, high_x, low_y, high_y, from_x, from_y, send_sem, recv_sem):
    gx, gy = lax.axis_index("gx"), lax.axis_index("gy")
    size_x, size_y = lax.axis_size("gx"), lax.axis_size("gy")
    barrier = pltpu.get_barrier_semaphore()

    def present(dx, dy):
        x, y = gx + dx, gy + dy
        return (x >= 0) & (x < size_x) & (y >= 0) & (y < size_y)

    def copy(k, dx, dy):
        if dy == 0:
            source = high_x if dx == 1 else low_x
            target = from_x.at[0 if dx == 1 else 1]
        else:
            source = high_y if dy == 1 else low_y
            target = from_y.at[1 - dx, 0 if dy == 1 else 1]
        return pltpu.make_async_remote_copy(
            src_ref=source,
            dst_ref=target,
            send_sem=send_sem.at[k],
            recv_sem=recv_sem.at[k],
            device_id={"gx": gx + dx, "gy": gy + dy},
            device_id_type=pl.DeviceIdType.MESH,
        )

    around = 0
    for dx, dy in ways():
        around = around + present(dx, dy).astype(jnp.int32)

        @pl.when(present(dx, dy))
        def _():
            pl.semaphore_signal(
                barrier,
                inc=1,
                device_id={"gx": gx + dx, "gy": gy + dy},
                device_id_type=pl.DeviceIdType.MESH,
            )

    pl.semaphore_wait(barrier, around)
    for k, (dx, dy) in enumerate(ways()):

        @pl.when(present(dx, dy))
        def _():
            copy(k, dx, dy).start()

    for k, (dx, dy) in enumerate(ways()):

        @pl.when(jnp.logical_not(present(-dx, -dy)))
        def _():
            if dy == 0:
                slot = 0 if dx == 1 else 1
                from_x[slot] = jnp.zeros(from_x.shape[1:], from_x.dtype)
            else:
                slot = 0 if dy == 1 else 1
                from_y[1 - dx, slot] = jnp.zeros(from_y.shape[2:], from_y.dtype)

    for k, (dx, dy) in enumerate(ways()):

        @pl.when(present(dx, dy))
        def _():
            copy(k, dx, dy).wait_send()

        @pl.when(present(-dx, -dy))
        def _():
            copy(k, dx, dy).wait_recv()


def halo(low_x, high_x, low_y, high_y, collective_id):
    return pl.pallas_call(
        halo_kernel,
        out_shape=[
            jax.ShapeDtypeStruct((2,) + low_x.shape, low_x.dtype),
            jax.ShapeDtypeStruct((3, 2) + low_y.shape, low_y.dtype),
        ],
        in_specs=[pl.BlockSpec(memory_space=pltpu.VMEM)] * 4,
        out_specs=[pl.BlockSpec(memory_space=pltpu.VMEM)] * 2,
        scratch_shapes=[pltpu.SemaphoreType.DMA((8,)), pltpu.SemaphoreType.DMA((8,))],
        compiler_params=pltpu.CompilerParams(
            collective_id=collective_id, has_side_effects=True
        ),
        name="halo",
    )(low_x, high_x, low_y, high_y)


def edge_columns(cy, width):
    row = lax.broadcasted_iota(jnp.int32, (2 * width, cy), 0)
    col = lax.broadcasted_iota(jnp.int32, (2 * width, cy), 1)
    return (col == jnp.where(row < width, row, row + cy - 2 * width)).astype(jnp.bfloat16)


def fields_kernel(
    members, most, note_ref, got_ref, c_ref, e_ref, coef_ref,
    x_ref, state_ref, sum_ref, ens_ref, run_ref,
):
    _, levels, cx, cy = e_ref.shape
    lev = c_ref.shape[1]
    fields = members + 1
    pieces, _, part, _ = state_ref.shape
    i = pl.program_id(0)

    @pl.when(i == 0)
    def _():
        home_sums(most, note_ref, got_ref, c_ref, sum_ref)

    for m in range(members):
        for l in range(levels):
            start = (m * levels + l) * cx
            ens_ref[start : start + cx, :] = e_ref[m, l].astype(jnp.float32)
    decay = jnp.exp(coef_ref[0])
    scale = coef_ref[1]
    state = [jnp.zeros((levels, cy), jnp.float32)] * fields
    for x in range(cx):
        base = sum_ref[pl.ds(x * lev + i * levels, levels), :] * scale
        for k in range(fields):
            value = base
            if k:
                value = base * ens_ref[pl.ds((k - 1) * levels * cx + x, levels, stride=cx), :]
            state[k] = value + decay * state[k]
            run_ref[k * cx + x] = state[k]
    for j in range(pieces):
        for k in range(fields):
            state_ref[j, k] = state[k][j * part : (j + 1) * part].astype(state_ref.dtype)
    state = [jnp.zeros((levels, cy), jnp.float32)] * fields
    for x in reversed(range(cx)):
        for k in range(fields):
            state[k] = run_ref[k * cx + x] + decay * state[k]
            x_ref[pl.ds(k * cx + x, levels, stride=fields * cx), :] = state[k]
    for j in range(pieces):
        for k in range(fields):
            state_ref[j, fields + k] = state[k][j * part : (j + 1) * part].astype(state_ref.dtype)


def carry_x_kernel(cells, s_ref, coef_ref, o_ref, in_ref, mid_ref, out_ref, sems):
    size = lax.axis_size("gx")
    me = lax.axis_index("gx")
    fields = s_ref.shape[1] // 2
    barrier = pltpu.get_barrier_semaphore()

    def greet(k, _):
        pl.semaphore_signal(
            barrier,
            inc=1,
            device_id={"gx": lax.rem(me + k, size)},
            device_id_type=pl.DeviceIdType.MESH,
        )
        return 0

    lax.fori_loop(1, size, greet, 0)
    in_ref[me] = s_ref[me]
    pl.semaphore_wait(barrier, size - 1)

    def copy(source, target, first, to, slot):
        return pltpu.make_async_remote_copy(
            src_ref=source.at[to],
            dst_ref=target.at[slot],
            send_sem=sems.at[first, to],
            recv_sem=sems.at[first + 1, slot],
            device_id={"gx": to},
            device_id_type=pl.DeviceIdType.MESH,
        )

    def swap(source, target, first):
        def send(k, _):
            copy(source, target, first, lax.rem(me + k, size), me).start()
            return 0

        def finish(k, _):
            peer = lax.rem(me + k, size)
            landed = copy(source, target, first, peer, peer)
            landed.wait_send()
            landed.wait_recv()
            return 0

        lax.fori_loop(1, size, send, 0)
        lax.fori_loop(1, size, finish, 0)

    swap(s_ref, in_ref, 0)
    rate = coef_ref[me, 0]
    step = jnp.exp(rate * cells)
    link = coef_ref[me, 2] * (jnp.exp(rate) - jnp.exp(rate * (2 * cells + 1)))
    for k in range(fields):
        enter = jnp.zeros(rate.shape, jnp.float32)
        entered = []
        for t in range(size):
            entered.append(enter)
            mid_ref[t, k] = enter.astype(mid_ref.dtype)
            enter = in_ref[t, k].astype(jnp.float32) + step * enter
        leave = jnp.zeros(rate.shape, jnp.float32)
        for t in reversed(range(size)):
            mid_ref[t, fields + k] = leave.astype(mid_ref.dtype)
            leave = in_ref[t, fields + k].astype(jnp.float32) + link * entered[t] + step * leave
    out_ref[me] = mid_ref[me]
    swap(mid_ref, out_ref, 2)
    parts, part = out_ref.shape[0], out_ref.shape[2]
    for t in range(parts):
        for k in range(2 * fields):
            o_ref[k, t * part : (t + 1) * part, :] = out_ref[t, k].astype(jnp.float32)


def rows_kernel(fields, x_ref, enter_ref, coef_ref, z_ref, state_ref, rows_ref, far_ref, sum_ref):
    levels, _, cy = z_ref.shape
    cx = z_ref.shape[1] // fields
    along = lax.broadcasted_iota(jnp.int32, (cx, cy), 0).astype(jnp.float32)

    @pl.when(pl.program_id(0) == 0)
    def _():
        row = lax.broadcasted_iota(jnp.int32, (cy, cy), 0)
        col = lax.broadcasted_iota(jnp.int32, (cy, cy), 1)
        far_ref[...] = jnp.abs(row - col).astype(jnp.float32)
        sum_ref[...] = (2 * cy - row - col).astype(jnp.float32)

    row = lax.broadcasted_iota(jnp.int32, (8, cy), 0)
    col = lax.broadcasted_iota(jnp.int32, (8, cy), 1)
    picks = (col == jnp.where(row == 0, cy - 1, jnp.where(row == 1, 0, -1))).astype(jnp.bfloat16)
    for l in range(levels):
        rate = coef_ref[0, l : l + 1, :]
        tall = coef_ref[2, l : l + 1, :]
        ahead = tall * (jnp.exp((along + 1.0) * rate) - jnp.exp((2.0 * cx + 1.0 - along) * rate))
        behind = jnp.exp((cx - along) * rate)
        parts = []
        for k in range(fields):
            parts.append(
                x_ref[l, k * cx : (k + 1) * cx, :]
                + ahead * enter_ref[k, l : l + 1, :]
                + behind * enter_ref[fields + k, l : l + 1, :]
            )
        high, low = split(jnp.concatenate(parts, axis=0))
        smooth = (
            coef_ref[1, l : l + 1, :]
            * tall
            * (jnp.exp(far_ref[...] * rate) - jnp.exp(sum_ref[...] * rate))
        )
        m_high, m_low = split(smooth)
        weights = jnp.concatenate(
            [
                jnp.concatenate([m_high, m_low], axis=1),
                jnp.concatenate([m_high, jnp.zeros_like(m_low)], axis=1),
            ],
            axis=0,
        )
        both = jnp.dot(
            jnp.concatenate([high, low], axis=1), weights, preferred_element_type=jnp.float32
        )
        z = both[:, :cy] + both[:, cy:]
        z_ref[l] = z
        ends = lax.dot_general(
            picks,
            z.astype(jnp.bfloat16),
            (((1,), (1,)), ((), ())),
            preferred_element_type=jnp.float32,
        )
        rows_ref[0, l : l + 1, :] = ends[0:1]
        rows_ref[1, l : l + 1, :] = ends[1:2]
    state_ref[...] = rows_ref[...].astype(state_ref.dtype)


def carry_y_kernel(cells, s_ref, coef_ref, o_ref, in_ref, sems):
    size = lax.axis_size("gy")
    me = lax.axis_index("gy")
    _, lev, width = s_ref.shape
    barrier = pltpu.get_barrier_semaphore()
    for k in range(1, size):
        pl.semaphore_signal(
            barrier,
            inc=1,
            device_id={"gy": lax.rem(me + k, size)},
            device_id_type=pl.DeviceIdType.MESH,
        )
    in_ref[me] = s_ref[...]
    pl.semaphore_wait(barrier, size - 1)

    def copy(to, slot):
        return pltpu.make_async_remote_copy(
            src_ref=s_ref,
            dst_ref=in_ref.at[slot],
            send_sem=sems.at[0, to],
            recv_sem=sems.at[1, slot],
            device_id={"gy": to},
            device_id_type=pl.DeviceIdType.MESH,
        )

    for k in range(1, size):
        copy(lax.rem(me + k, size), me).start()
    for k in range(1, size):
        peer = lax.rem(me + k, size)
        landed = copy(peer, peer)
        landed.wait_send()
        landed.wait_recv()
    rate = coef_ref[0, :, 0:1]
    step = jnp.broadcast_to(jnp.exp(rate * cells), (lev, width))
    link = coef_ref[2, :, 0:1] * (jnp.exp(rate) - jnp.exp(rate * (2 * cells + 1)))
    link = jnp.broadcast_to(link, (lev, width))
    enter = jnp.zeros((lev, width), jnp.float32)
    mine = enter
    entered = []
    for t in range(size):
        entered.append(enter)
        mine = jnp.where(me == t, enter, mine)
        enter = in_ref[t, 0].astype(jnp.float32) + step * enter
    leave = jnp.zeros((lev, width), jnp.float32)
    last = leave
    for t in reversed(range(size)):
        last = jnp.where(me == t, leave, last)
        leave = in_ref[t, 1].astype(jnp.float32) + link * entered[t] + step * leave
    o_ref[0] = mine
    o_ref[1] = last


def ends_of(first, second):
    row = lax.broadcasted_iota(jnp.int32, (8, first.shape[1]), 0)
    parts = [jnp.broadcast_to(v, row.shape) for v in (first, second)]
    (a, b), (c, d) = [[p.astype(jnp.float32) for p in split(v)] for v in parts]
    return row, a, b, c, d


def final_kernel(
    members, z_ref, y_ref, coef_ref, u_ref, v_ref,
    a_ref, s_ref, low_x, high_x, low_y, high_y,
):
    _, levels, cx, cy = a_ref.shape
    columns = edge_columns(cy, STRIP)
    along = lax.broadcasted_iota(jnp.int32, (1, cy), 1).astype(jnp.float32)
    for l in range(levels):
        rate = coef_ref[0, l : l + 1, :]
        tall = coef_ref[2, l : l + 1, :]
        ahead = tall * (jnp.exp((along + 1.0) * rate) - jnp.exp((2.0 * cy + 1.0 - along) * rate))
        behind = jnp.exp((cy - along) * rate)
        row, a, b, c, d = ends_of(ahead, behind)
        across = jnp.where(row < 2, a, jnp.where(row == 2, b, jnp.where(row < 5, c, d)))
        row, a, b, c, d = ends_of(y_ref[0, l : l + 1, :], y_ref[1, l : l + 1, :])
        down = jnp.where(row % 3 == 1, jnp.where(row < 3, b, d), jnp.where(row < 3, a, c))
        down = jnp.where(row < 6, down, 0.0)
        field = z_ref[l] + lax.dot_general(
            down.astype(jnp.bfloat16),
            across.astype(jnp.bfloat16),
            (((0,), (0,)), ((), ())),
            preferred_element_type=jnp.float32,
        )
        static = field[:cx]
        s_ref[l] = static
        for m in range(members):
            a_ref[m, l] = field[(m + 1) * cx : (m + 2) * cx]
        for k, value in enumerate((static.astype(jnp.bfloat16), u_ref[l], v_ref[l])):
            low_x[k, l] = value[:STRIP]
            high_x[k, l] = value[cx - STRIP :]
            sides = lax.dot_general(
                columns, value, (((1,), (1,)), ((), ())), preferred_element_type=jnp.float32
            )
            low_y[k, l] = sides[:STRIP].astype(low_y.dtype)
            high_y[k, l] = sides[STRIP:].astype(high_y.dtype)


def transport_kernel(s_ref, u_ref, v_ref, hx_ref, hy_ref, o_ref):
    levels, cx, cy = o_ref.shape
    rows, lanes = cx + 2 * EDGE, 2 * cy
    blank = jnp.zeros((EDGE - STRIP, cy), jnp.float32)
    place = edge_columns(cy, STRIP)

    def widened(value, k, l):
        strips = []
        for j in range(3):
            pair = jnp.concatenate(
                [
                    hy_ref[j, 1, k, l].astype(jnp.float32),
                    hy_ref[j, 0, k, l].astype(jnp.float32),
                ],
                axis=0,
            ).astype(jnp.bfloat16)
            strips.append(
                lax.dot_general(
                    pair, place, (((0,), (0,)), ((), ())), preferred_element_type=jnp.float32
                )
            )
        above = hx_ref[0, k, l].astype(jnp.float32)
        below = hx_ref[1, k, l].astype(jnp.float32)
        return jnp.concatenate(
            [
                jnp.concatenate([blank, above, value, below, blank], axis=0),
                jnp.concatenate([strips[0][cx - EDGE :], strips[1], strips[2][:EDGE]], axis=0),
            ],
            axis=1,
        )

    for l in range(levels):
        s = widened(s_ref[l], 0, l)
        u = widened(u_ref[l].astype(jnp.float32), 1, l)
        v = widened(v_ref[l].astype(jnp.float32), 2, l)
        east, north = u > 0.0, v > 0.0
        u, v = jnp.abs(u), jnp.abs(v)
        for _ in range(HALO):
            s = s + u * (jnp.where(east, pltpu.roll(s, 1, 0), pltpu.roll(s, rows - 1, 0)) - s)
            s = s + v * (jnp.where(north, pltpu.roll(s, 1, 1), pltpu.roll(s, lanes - 1, 1)) - s)
        o_ref[l] = s[EDGE : EDGE + cx, :cy]


def body(
    increment,
    ensemble,
    wind_u,
    wind_v,
    filter_length,
    jacobian,
    obs_weight,
    departure,
    obs_home,
    obs_line,
    obs_count,
):
    axes = ("gx", "gy")
    home_count = lax.axis_size(axes)
    records_here = obs_home.shape[0]
    most = (records_here + home_count - 1) // home_count
    lev, cx, cy = increment.shape
    members = ensemble.shape[0]
    fields = members + 1
    slot_count = home_count * most
    index = jnp.arange(records_here, dtype=jnp.int32)
    earlier = (obs_home[:, None] == obs_home[None, :]) & (index[None, :] < index[:, None])
    slot_of = obs_home * most + jnp.sum(earlier.astype(jnp.int32), axis=1)
    placing = slot_of[:, None] == jnp.arange(slot_count, dtype=jnp.int32)[None, :]
    order, lines, counts = [
        jnp.sum(jnp.where(placing, value[:, None], 0), axis=0)
        for value in (index, obs_line, obs_count)
    ]
    got, note = observe(
        order, lines, counts, jacobian[0], obs_weight, departure, axes, most, 3
    )
    across = jnp.transpose(increment, (1, 0, 2))
    rate = -1.0 / filter_length
    tall = -1.0 / jnp.expm1(2.0 * rate)
    gain = -jnp.expm1(rate) * jnp.sqrt(-jnp.expm1(2.0 * rate))
    coef = jnp.broadcast_to(jnp.stack([rate, gain, tall])[:, :, None], (3, lev, cy))
    size_x, size_y = lax.axis_size("gx"), lax.axis_size("gy")
    part = lev // size_x
    tile = 8
    steps = lev // tile
    pieces = tile // part

    def levels_first(*shape):
        return pl.BlockSpec((tile,) + shape, lambda i: (i, 0, 0))

    def levels_second(*shape):
        first, *rest = shape
        return pl.BlockSpec((first, tile) + tuple(rest), lambda i: (0, i) + (0,) * len(rest))

    def whole(array):
        return pl.BlockSpec(
            array.shape, lambda i: (0,) * array.ndim, pipeline_mode=pl.Buffered(1)
        )

    params = pltpu.CompilerParams(
        dimension_semantics=("arbitrary",), vmem_limit_bytes=56 * 1024 * 1024
    )
    rows = fields * cx
    local, state_x = pl.pallas_call(
        functools.partial(fields_kernel, members, most),
        grid=(steps,),
        in_specs=[
            pl.BlockSpec(memory_space=pltpu.SMEM),
            whole(got),
            whole(across),
            levels_second(members, cx, cy),
            levels_second(3, cy),
        ],
        out_specs=[
            pl.BlockSpec((tile * rows, cy), lambda i: (i, 0)),
            pl.BlockSpec((pieces, 2 * fields, part, cy), lambda i: (i, 0, 0, 0)),
        ],
        out_shape=[
            jax.ShapeDtypeStruct((lev * rows, cy), jnp.float32),
            jax.ShapeDtypeStruct((size_x, 2 * fields, part, cy), jnp.bfloat16),
        ],
        scratch_shapes=[
            pltpu.VMEM((cx * lev, cy), jnp.float32),
            pltpu.VMEM((members * tile * cx, cy), jnp.float32),
            pltpu.VMEM((rows, tile, cy), jnp.float32),
        ],
        compiler_params=params,
        name="fields",
    )(note, got, across, ensemble, coef)
    local = local.reshape(lev, rows, cy)

    vmem = pl.BlockSpec(memory_space=pltpu.VMEM)
    split_coef = jnp.moveaxis(coef.reshape(3, size_x, part, cy), 1, 0)
    swept = pl.pallas_call(
        functools.partial(carry_x_kernel, cx),
        out_shape=jax.ShapeDtypeStruct((2 * fields, lev, cy), jnp.float32),
        in_specs=[vmem, vmem],
        out_specs=vmem,
        scratch_shapes=[pltpu.VMEM(state_x.shape, jnp.bfloat16)] * 3
        + [pltpu.SemaphoreType.DMA((4, size_x))],
        compiler_params=pltpu.CompilerParams(collective_id=1, has_side_effects=True),
        name="carry_x",
    )(state_x, split_coef)

    z, state_y = pl.pallas_call(
        functools.partial(rows_kernel, fields),
        grid=(steps,),
        in_specs=[levels_first(rows, cy), levels_second(2 * fields, cy), levels_second(3, cy)],
        out_specs=[levels_first(rows, cy), levels_second(2, rows)],
        out_shape=[
            jax.ShapeDtypeStruct((lev, rows, cy), jnp.float32),
            jax.ShapeDtypeStruct((2, lev, rows), jnp.bfloat16),
        ],
        scratch_shapes=[
            pltpu.VMEM((2, tile, rows), jnp.float32),
            pltpu.VMEM((cy, cy), jnp.float32),
            pltpu.VMEM((cy, cy), jnp.float32),
        ],
        compiler_params=params,
        name="rows",
    )(local, swept, coef)

    entered = pl.pallas_call(
        functools.partial(carry_y_kernel, cy),
        out_shape=jax.ShapeDtypeStruct((2, lev, rows), jnp.float32),
        in_specs=[vmem, vmem],
        out_specs=vmem,
        scratch_shapes=[
            pltpu.VMEM((size_y, 2, lev, rows), jnp.bfloat16),
            pltpu.SemaphoreType.DMA((2, size_y)),
        ],
        compiler_params=pltpu.CompilerParams(collective_id=2, has_side_effects=True),
        name="carry_y",
    )(state_y, coef)

    grad_alpha, static, *strips = pl.pallas_call(
        functools.partial(final_kernel, members),
        grid=(steps,),
        in_specs=[
            levels_first(rows, cy),
            levels_second(2, rows),
            levels_second(3, cy),
            levels_first(cx, cy),
            levels_first(cx, cy),
        ],
        out_specs=[
            levels_second(members, cx, cy),
            levels_first(cx, cy),
            levels_second(3, STRIP, cy),
            levels_second(3, STRIP, cy),
            levels_second(3, STRIP, cx),
            levels_second(3, STRIP, cx),
        ],
        out_shape=[
            jax.ShapeDtypeStruct((members, lev, cx, cy), jnp.float32),
            jax.ShapeDtypeStruct((lev, cx, cy), jnp.float32),
            jax.ShapeDtypeStruct((3, lev, STRIP, cy), jnp.bfloat16),
            jax.ShapeDtypeStruct((3, lev, STRIP, cy), jnp.bfloat16),
            jax.ShapeDtypeStruct((3, lev, STRIP, cx), jnp.bfloat16),
            jax.ShapeDtypeStruct((3, lev, STRIP, cx), jnp.bfloat16),
        ],
        compiler_params=params,
        name="final",
    )(z, entered, coef, wind_u, wind_v)

    halo_x, halo_y = halo(*strips, 5)
    static = pl.pallas_call(
        transport_kernel,
        grid=(steps,),
        in_specs=[
            levels_first(cx, cy),
            levels_first(cx, cy),
            levels_first(cx, cy),
            pl.BlockSpec((2, 3, tile, STRIP, cy), lambda i: (0, 0, i, 0, 0)),
            pl.BlockSpec((3, 2, 3, tile, STRIP, cx), lambda i: (0, 0, 0, i, 0, 0)),
        ],
        out_specs=levels_first(cx, cy),
        out_shape=jax.ShapeDtypeStruct((lev, cx, cy), jnp.float32),
        compiler_params=params,
        name="transport",
    )(static, wind_u, wind_v, halo_x, halo_y)
    return (grad_alpha, static)


def solution(mesh):
    return jax.shard_map(
        body,
        mesh=mesh,
        in_specs=(
            P(None, "gx", "gy"),
            P(None, None, "gx", "gy"),
            P(None, "gx", "gy"),
            P(None, "gx", "gy"),
            P(),
            P(("gx", "gy"), None, None),
            P(("gx", "gy"), None),
            P(("gx", "gy"), None, None),
            P(("gx", "gy")),
            P(("gx", "gy")),
            P(("gx", "gy")),
        ),
        out_specs=(P(None, None, "gx", "gy"), P(None, "gx", "gy")),
        check_vma=False,
    )
```

```python
import functools
import jax
import jax.numpy as jnp
from jax import lax
from jax.experimental import pallas as pl
from jax.experimental.pallas import tpu as pltpu
from jax.sharding import PartitionSpec as P

HALO = 3
CODE = 32767.0
highest = lax.Precision.HIGHEST


def peer_id(axes, index):
    if len(axes) == 1:
        return {axes[0]: index}
    minor = lax.axis_size(axes[1])
    return {axes[0]: index // minor, axes[1]: index % minor}


def split(value):
    high = value.astype(jnp.bfloat16)
    return high, (value - high.astype(jnp.float32)).astype(jnp.bfloat16)


def position(axes):
    me = lax.axis_index(axes[0])
    for name in axes[1:]:
        me = me * lax.axis_size(name) + lax.axis_index(name)
    return me


def coded(value):
    top = jnp.max(jnp.max(jnp.abs(value), axis=1, keepdims=True), axis=0, keepdims=True)
    top = jnp.maximum(top, 1e-30)
    code = jnp.round(value * (CODE / top)).astype(jnp.int32).astype(jnp.int16)
    return code, top * (1.0 / CODE)


def obs_kernel(
    axes, most, order_ref, line_ref, count_ref, j_ref, w_ref, d_hbm, got_ref, note_ref,
    d_buf, send_buf, note_buf, lhs_ref, hold_ref, scale_ref,
    d_sem, send_sem, recv_sem, note_send, note_recv,
):
    count = lax.axis_size(axes)
    half = count // 2
    me = position(axes)
    lev = j_ref.shape[1]
    cy = d_buf.shape[2]
    barrier = pltpu.get_barrier_semaphore()
    pieces = d_sem.shape[0]
    size = d_buf.shape[0] // pieces

    def piece(i):
        rows = pl.ds(i * size, size)
        return pltpu.make_async_copy(d_hbm.at[rows], d_buf.at[rows], d_sem.at[i])

    for i in range(pieces):
        piece(i).start()

    def greet(k, _):
        pl.semaphore_signal(
            barrier,
            inc=1,
            device_id=peer_id(axes, lax.rem(me + k, count)),
            device_id_type=pl.DeviceIdType.MESH,
        )
        return 0

    lax.fori_loop(1, count, greet, 0)
    turned = j_ref[...].astype(jnp.float32).T
    high, low = split(turned * w_ref[...])
    lhs_ref[...] = jnp.concatenate([high, low], axis=0)
    both = jnp.dot(lhs_ref[...], j_ref[...], preferred_element_type=jnp.float32)
    normal = both[:lev] + both[lev:]
    code, scale = coded(normal)
    hold_ref[...] = jnp.concatenate([code[: lev // 2], code[lev // 2 :]], axis=1)
    scale_ref[...] = jnp.broadcast_to(scale, scale_ref.shape)
    for i in range(pieces):
        piece(i).wait()
    pl.semaphore_wait(barrier, count - 1)
    lane = lax.broadcasted_iota(jnp.int32, (1, cy), 1)

    def fill(home, target, note):
        blocks = [d_buf[order_ref[home * most + m]] for m in range(most)]
        both = jnp.dot(
            lhs_ref[...], jnp.concatenate(blocks, axis=1), preferred_element_type=jnp.float32
        )
        word = jnp.where(lane == 3 * most, scale_ref[0:1, :], 0.0)
        for m in range(most):
            part = both[:lev, m * cy : (m + 1) * cy] + both[lev:, m * cy : (m + 1) * cy]
            code, scale = coded(part)
            target[m * lev : (m + 1) * lev, :] = code
            word = jnp.where(lane == m, line_ref[home * most + m].astype(jnp.float32), word)
            word = jnp.where(lane == most + m, count_ref[home * most + m].astype(jnp.float32), word)
            word = jnp.where(lane == 2 * most + m, scale, word)
        target[most * lev :, :] = hold_ref[...]
        note[...] = word

    def goal(t):
        j = t + t // half
        mine, place = me // half, lax.rem(me, half)
        other = lax.rem(mine + 1 + j // half, 2)
        return other * half + lax.rem(place + j, half)

    def sends(to, origin):
        peer = dict(device_id=peer_id(axes, to), device_id_type=pl.DeviceIdType.MESH)
        return (
            pltpu.make_async_remote_copy(
                src_ref=send_buf.at[to], dst_ref=got_ref.at[origin],
                send_sem=send_sem.at[to], recv_sem=recv_sem.at[origin], **peer
            ),
            pltpu.make_async_remote_copy(
                src_ref=note_buf.at[to], dst_ref=note_ref.at[origin],
                send_sem=note_send.at[to], recv_sem=note_recv.at[origin], **peer
            ),
        )

    def begin(to):
        for copy in sends(to, me):
            copy.start()

    first = goal(0)
    fill(first, send_buf.at[first], note_buf.at[first])

    def step(t, _):
        to = goal(t)
        fill(to, send_buf.at[to], note_buf.at[to])
        begin(goal(t - 1))
        return 0

    lax.fori_loop(1, count - 1, step, 0)
    fill(me, got_ref.at[me], note_ref.at[me])
    begin(goal(count - 2))

    def finish(k, _):
        peer = lax.rem(me + k, count)
        for copy in sends(peer, peer):
            copy.wait_send()
            copy.wait_recv()
        return 0

    lax.fori_loop(1, count, finish, 0)


def observe(order, lines, counts, jacobian, weight, departure, axes, most, collective_id):
    count = lax.axis_size(axes)
    channels, lev = jacobian.shape
    records, _, cy = departure.shape
    rows = most * lev + lev // 2
    smem = pl.BlockSpec(memory_space=pltpu.SMEM)
    vmem = pl.BlockSpec(memory_space=pltpu.VMEM)
    dma = pltpu.SemaphoreType.DMA
    return pl.pallas_call(
        functools.partial(obs_kernel, axes, most),
        out_shape=[
            jax.ShapeDtypeStruct((count, rows, cy), jnp.int16),
            jax.ShapeDtypeStruct((count, 1, cy), jnp.float32),
        ],
        in_specs=[smem, smem, smem, vmem, vmem, pl.BlockSpec(memory_space=pl.ANY)],
        out_specs=[vmem, vmem],
        scratch_shapes=[
            pltpu.VMEM((records, channels, cy), jnp.bfloat16),
            pltpu.VMEM((count, rows, cy), jnp.int16),
            pltpu.VMEM((count, 1, cy), jnp.float32),
            pltpu.VMEM((2 * lev, channels), jnp.bfloat16),
            pltpu.VMEM((lev // 2, 2 * lev), jnp.int16),
            pltpu.VMEM((8, cy), jnp.float32),
            dma((8,)), dma((count,)), dma((count,)), dma((count,)), dma((count,)),
        ],
        compiler_params=pltpu.CompilerParams(
            collective_id=collective_id,
            has_side_effects=True,
            vmem_limit_bytes=56 * 1024 * 1024,
        ),
        name="observe",
    )(order, lines, counts, jacobian, weight, departure)


def home_sums(most, note_ref, got_ref, c_ref, sum_ref):
    homes = got_ref.shape[0]
    lev, cy = c_ref.shape[1:]
    sum_ref[...] = jnp.zeros(sum_ref.shape, sum_ref.dtype)
    lane = lax.broadcasted_iota(jnp.int32, (lev // 2, 2 * lev), 1)
    column = lax.broadcasted_iota(jnp.int32, (lev, cy), 1)

    def one(k, _):
        code = got_ref[k, most * lev :, :].astype(jnp.int32).astype(jnp.float32)
        high, low = split(code)
        high, low = high.astype(jnp.float32), low.astype(jnp.float32)
        matrix = jnp.concatenate(
            [
                jnp.where(lane < lev, high, pltpu.roll(low, lev, 1)),
                jnp.where(lane < lev, pltpu.roll(high, lev, 1), low),
            ],
            axis=0,
        ).astype(jnp.bfloat16)
        lines = [note_ref[k, 0, m].astype(jnp.int32) for m in range(most)]
        block = jnp.concatenate([c_ref[line] for line in lines], axis=1)
        product = jnp.dot(
            matrix, jnp.concatenate([block, block], axis=0), preferred_element_type=jnp.float32
        )
        for m in range(most):
            part = got_ref[k, m * lev : (m + 1) * lev, :].astype(jnp.int32).astype(jnp.float32)
            value = (
                note_ref[k, 0, 3 * most] * product[:, m * cy : (m + 1) * cy]
                - note_ref[k, 0, 2 * most + m] * part
            )
            value = jnp.where(column < note_ref[k, 0, most + m].astype(jnp.int32), value, 0.0)
            rows = pl.ds(pl.multiple_of(lines[m] * lev, lev), lev)
            sum_ref[rows, :] += value
        return 0

    lax.fori_loop(0, homes, one, 0)


def ways():
    return [(dx, dy) for dx in (-1, 0, 1) for dy in (-1, 0, 1) if (dx, dy) != (0, 0)]


class Edges:
    def __init__(self, edge_ref, strip_ref, rows_ref, strips_ref, sems):
        self.refs = edge_ref, strip_ref, rows_ref, strips_ref
        self.sems = sems
        self.at = lax.axis_index("gx"), lax.axis_index("gy")
        self.size = lax.axis_size("gx"), lax.axis_size("gy")

    def present(self, dx, dy):
        x, y = self.at[0] + dx, self.at[1] + dy
        return (x >= 0) & (x < self.size[0]) & (y >= 0) & (y < self.size[1])

    def copies(self, k, dx, dy):
        edge_ref, strip_ref, rows_ref, strips_ref = self.refs
        cx = strip_ref.shape[1]
        slot = 1 - dy
        if dx == 0:
            pairs = [(strip_ref, strips_ref.at[slot, :, pl.ds(HALO, cx)])]
        else:
            first = cx - HALO if dx == 1 else 0
            target = 0 if dx == 1 else cx + HALO
            pairs = [
                (
                    strip_ref.at[:, pl.ds(first, HALO)],
                    strips_ref.at[slot, :, pl.ds(target, HALO)],
                )
            ]
            if dy == 0:
                side = 0 if dx == 1 else 1
                pairs.append((edge_ref.at[1 - side], rows_ref.at[side]))
        return [
            pltpu.make_async_remote_copy(
                src_ref=source,
                dst_ref=target,
                send_sem=self.sems.at[0, j, k],
                recv_sem=self.sems.at[1, j, k],
                device_id={"gx": self.at[0] + dx, "gy": self.at[1] + dy},
                device_id_type=pl.DeviceIdType.MESH,
            )
            for j, (source, target) in enumerate(pairs)
        ]

    def greet(self, barrier):
        around = 0
        for dx, dy in ways():
            here = self.present(dx, dy)
            around = around + here.astype(jnp.int32)

            @pl.when(here)
            def _():
                pl.semaphore_signal(
                    barrier,
                    inc=1,
                    device_id={"gx": self.at[0] + dx, "gy": self.at[1] + dy},
                    device_id_type=pl.DeviceIdType.MESH,
                )

        return around

    def send(self):
        _, strip_ref, rows_ref, strips_ref = self.refs
        for k, (dx, dy) in enumerate(ways()):

            @pl.when(self.present(dx, dy))
            def _():
                for copy in self.copies(k, dx, dy):
                    copy.start()

        cx = strip_ref.shape[1]
        strips_ref[1, :, HALO : HALO + cx] = strip_ref[...]
        for dx, dy in ways():
            rows = HALO if dx else cx
            first = HALO if dx == 0 else 0 if dx == 1 else cx + HALO

            @pl.when(jnp.logical_not(self.present(-dx, -dy)))
            def _():
                blank = strips_ref[1 - dy, :, first : first + rows]
                strips_ref[1 - dy, :, first : first + rows] = jnp.zeros(blank.shape, blank.dtype)
                if dy == 0:
                    side = 0 if dx == 1 else 1
                    rows_ref[side] = jnp.zeros(rows_ref.shape[1:], rows_ref.dtype)

    def finish(self):
        for k, (dx, dy) in enumerate(ways()):

            @pl.when(self.present(dx, dy))
            def _():
                for copy in self.copies(k, dx, dy):
                    copy.wait_send()

            @pl.when(self.present(-dx, -dy))
            def _():
                for copy in self.copies(k, dx, dy):
                    copy.wait_recv()


def edge_shapes(arrays, lev, cx, cy):
    return [
        jax.ShapeDtypeStruct((2, arrays, HALO, lev, cy), jnp.bfloat16),
        jax.ShapeDtypeStruct((3, arrays, cx + 2 * HALO, 8, cy), jnp.bfloat16),
    ]


def halo_kernel(edge_ref, strip_ref, rows_ref, strips_ref, sems):
    edges = Edges(edge_ref, strip_ref, rows_ref, strips_ref, sems)
    barrier = pltpu.get_barrier_semaphore()
    around = edges.greet(barrier)
    pl.semaphore_wait(barrier, around)
    edges.send()
    edges.finish()


def put_strip(turned_ref, strip_ref, w, group):
    width = turned_ref.shape[1] // pl.num_programs(0)
    value = turned_ref[...]
    lane = lax.broadcasted_iota(jnp.int32, value.shape, 1)
    first = group * width
    moved = pltpu.roll(value, first + width // 4, 1)
    here = (lane >= first) & (lane < first + width // 2)
    strip_ref[w] = jnp.where(here, moved, strip_ref[w])


def turn(value_ref, out_ref, edge_ref, strips_ref, turned_ref, strip_ref, w, group):
    levels, cx, cy = value_ref.shape
    for l in range(levels):
        turned_ref[pl.ds(l, cx, stride=levels), :] = value_ref[l].astype(jnp.float32)
    turned = turned_ref[...].reshape(cx, levels, cy)
    out_ref[...] = turned.astype(out_ref.dtype)
    edge_ref[0, w] = turned[:HALO].astype(edge_ref.dtype)
    edge_ref[1, w] = turned[cx - HALO :].astype(edge_ref.dtype)

    @pl.when(group == 0)
    def _():
        strip_ref[w] = jnp.zeros(strip_ref.shape[1:], strip_ref.dtype)

    put_strip(turned_ref, strip_ref, w, group)

    @pl.when(group == pl.num_programs(0) - 1)
    def _():
        strips_ref[w] = strip_ref[w].reshape(cx, levels, cy).astype(strips_ref.dtype)


def fields_kernel(
    members, most, note_ref, got_ref, c_ref, e_ref, coef_ref, u_ref, v_ref,
    x_ref, state_ref, ut_ref, vt_ref, edge_ref, strips_ref,
    sum_ref, ens_ref, run_ref, turned_ref, strip_ref,
):
    _, levels, cx, cy = e_ref.shape
    lev = c_ref.shape[1]
    fields = members + 1
    pieces, _, part, _ = state_ref.shape
    i = pl.program_id(0)

    @pl.when(i == 0)
    def _():
        home_sums(most, note_ref, got_ref, c_ref, sum_ref)

    for w, (wind_ref, wt_ref) in enumerate(((u_ref, ut_ref), (v_ref, vt_ref))):
        turn(wind_ref, wt_ref, edge_ref, strips_ref, turned_ref, strip_ref, w, i)
    for m in range(members):
        for l in range(levels):
            start = (m * levels + l) * cx
            ens_ref[start : start + cx, :] = e_ref[m, l].astype(jnp.float32)
    decay = jnp.exp(coef_ref[0])
    scale = coef_ref[1]
    state = [jnp.zeros((levels, cy), jnp.float32)] * fields
    for x in range(cx):
        base = sum_ref[pl.ds(x * lev + i * levels, levels), :] * scale
        for k in range(fields):
            value = base
            if k:
                value = base * ens_ref[pl.ds((k - 1) * levels * cx + x, levels, stride=cx), :]
            state[k] = value + decay * state[k]
            run_ref[k * cx + x] = state[k]
    for j in range(pieces):
        for k in range(fields):
            state_ref[j, k] = state[k][j * part : (j + 1) * part].astype(state_ref.dtype)
    state = [jnp.zeros((levels, cy), jnp.float32)] * fields
    for x in reversed(range(cx)):
        for k in range(fields):
            state[k] = run_ref[k * cx + x] + decay * state[k]
            x_ref[pl.ds(k * cx + x, levels, stride=fields * cx), :] = state[k]
    for j in range(pieces):
        for k in range(fields):
            state_ref[j, fields + k] = state[k][j * part : (j + 1) * part].astype(state_ref.dtype)


def carry_x_kernel(cells, s_ref, coef_ref, o_ref, in_ref, mid_ref, out_ref, sems):
    size = lax.axis_size("gx")
    me = lax.axis_index("gx")
    fields = s_ref.shape[1] // 2
    barrier = pltpu.get_barrier_semaphore()

    def greet(k, _):
        pl.semaphore_signal(
            barrier,
            inc=1,
            device_id={"gx": lax.rem(me + k, size)},
            device_id_type=pl.DeviceIdType.MESH,
        )
        return 0

    lax.fori_loop(1, size, greet, 0)
    in_ref[me] = s_ref[me]
    pl.semaphore_wait(barrier, size - 1)

    def copy(source, target, first, to, slot):
        return pltpu.make_async_remote_copy(
            src_ref=source.at[to],
            dst_ref=target.at[slot],
            send_sem=sems.at[first, to],
            recv_sem=sems.at[first + 1, slot],
            device_id={"gx": to},
            device_id_type=pl.DeviceIdType.MESH,
        )

    def swap(source, target, first):
        def send(k, _):
            copy(source, target, first, lax.rem(me + k, size), me).start()
            return 0

        def finish(k, _):
            peer = lax.rem(me + k, size)
            landed = copy(source, target, first, peer, peer)
            landed.wait_send()
            landed.wait_recv()
            return 0

        lax.fori_loop(1, size, send, 0)
        lax.fori_loop(1, size, finish, 0)

    swap(s_ref, in_ref, 0)
    rate = coef_ref[me, 0]
    step = jnp.exp(rate * cells)
    link = coef_ref[me, 2] * (jnp.exp(rate) - jnp.exp(rate * (2 * cells + 1)))
    for k in range(fields):
        enter = jnp.zeros(rate.shape, jnp.float32)
        entered = []
        for t in range(size):
            entered.append(enter)
            mid_ref[t, k] = enter.astype(mid_ref.dtype)
            enter = in_ref[t, k].astype(jnp.float32) + step * enter
        leave = jnp.zeros(rate.shape, jnp.float32)
        for t in reversed(range(size)):
            mid_ref[t, fields + k] = leave.astype(mid_ref.dtype)
            leave = in_ref[t, fields + k].astype(jnp.float32) + link * entered[t] + step * leave
    out_ref[me] = mid_ref[me]
    swap(mid_ref, out_ref, 2)
    parts, part = out_ref.shape[0], out_ref.shape[2]
    for t in range(parts):
        for k in range(2 * fields):
            o_ref[k, t * part : (t + 1) * part, :] = out_ref[t, k].astype(jnp.float32)


def rows_kernel(fields, x_ref, enter_ref, coef_ref, z_ref, state_ref, rows_ref, far_ref, sum_ref):
    levels, _, cy = z_ref.shape
    cx = z_ref.shape[1] // fields
    along = lax.broadcasted_iota(jnp.int32, (cx, cy), 0).astype(jnp.float32)

    @pl.when(pl.program_id(0) == 0)
    def _():
        row = lax.broadcasted_iota(jnp.int32, (cy, cy), 0)
        col = lax.broadcasted_iota(jnp.int32, (cy, cy), 1)
        far_ref[...] = jnp.abs(row - col).astype(jnp.float32)
        sum_ref[...] = (2 * cy - row - col).astype(jnp.float32)

    row = lax.broadcasted_iota(jnp.int32, (8, cy), 0)
    col = lax.broadcasted_iota(jnp.int32, (8, cy), 1)
    picks = (col == jnp.where(row == 0, cy - 1, jnp.where(row == 1, 0, -1))).astype(jnp.bfloat16)
    for l in range(levels):
        rate = coef_ref[0, l : l + 1, :]
        tall = coef_ref[2, l : l + 1, :]
        ahead = tall * (jnp.exp((along + 1.0) * rate) - jnp.exp((2.0 * cx + 1.0 - along) * rate))
        behind = jnp.exp((cx - along) * rate)
        parts = []
        for k in range(fields):
            parts.append(
                x_ref[l, k * cx : (k + 1) * cx, :]
                + ahead * enter_ref[k, l : l + 1, :]
                + behind * enter_ref[fields + k, l : l + 1, :]
            )
        high, low = split(jnp.concatenate(parts, axis=0))
        smooth = (
            coef_ref[1, l : l + 1, :]
            * tall
            * (jnp.exp(far_ref[...] * rate) - jnp.exp(sum_ref[...] * rate))
        )
        m_high, m_low = split(smooth)
        weights = jnp.concatenate(
            [
                jnp.concatenate([m_high, m_low], axis=1),
                jnp.concatenate([m_high, jnp.zeros_like(m_low)], axis=1),
            ],
            axis=0,
        )
        both = jnp.dot(
            jnp.concatenate([high, low], axis=1), weights, preferred_element_type=jnp.float32
        )
        z = both[:, :cy] + both[:, cy:]
        z_ref[l] = z
        ends = lax.dot_general(
            picks,
            z.astype(jnp.bfloat16),
            (((1,), (1,)), ((), ())),
            preferred_element_type=jnp.float32,
        )
        rows_ref[0, l : l + 1, :] = ends[0:1]
        rows_ref[1, l : l + 1, :] = ends[1:2]
    state_ref[...] = rows_ref[...].astype(state_ref.dtype)


def carry_y_kernel(
    cells, s_ref, coef_ref, edge_ref, strip_ref, o_ref, rows_ref, strips_ref, in_ref, sems, more
):
    edges = Edges(edge_ref, strip_ref, rows_ref, strips_ref, more)
    size = lax.axis_size("gy")
    me = lax.axis_index("gy")
    _, lev, width = s_ref.shape
    barrier = pltpu.get_barrier_semaphore()
    for k in range(1, size):
        pl.semaphore_signal(
            barrier,
            inc=1,
            device_id={"gy": lax.rem(me + k, size)},
            device_id_type=pl.DeviceIdType.MESH,
        )
    around = edges.greet(barrier)
    in_ref[me] = s_ref[...]
    pl.semaphore_wait(barrier, size - 1 + around)

    def copy(to, slot):
        return pltpu.make_async_remote_copy(
            src_ref=s_ref,
            dst_ref=in_ref.at[slot],
            send_sem=sems.at[0, to],
            recv_sem=sems.at[1, slot],
            device_id={"gy": to},
            device_id_type=pl.DeviceIdType.MESH,
        )

    for k in range(1, size):
        copy(lax.rem(me + k, size), me).start()
    edges.send()
    for k in range(1, size):
        peer = lax.rem(me + k, size)
        landed = copy(peer, peer)
        landed.wait_send()
        landed.wait_recv()
    rate = coef_ref[0, :, 0:1]
    step = jnp.broadcast_to(jnp.exp(rate * cells), (lev, width))
    link = coef_ref[2, :, 0:1] * (jnp.exp(rate) - jnp.exp(rate * (2 * cells + 1)))
    link = jnp.broadcast_to(link, (lev, width))
    enter = jnp.zeros((lev, width), jnp.float32)
    mine = enter
    entered = []
    for t in range(size):
        entered.append(enter)
        mine = jnp.where(me == t, enter, mine)
        enter = in_ref[t, 0].astype(jnp.float32) + step * enter
    leave = jnp.zeros((lev, width), jnp.float32)
    last = leave
    for t in reversed(range(size)):
        last = jnp.where(me == t, leave, last)
        leave = in_ref[t, 1].astype(jnp.float32) + link * entered[t] + step * leave
    o_ref[0] = mine
    o_ref[1] = last
    edges.finish()


def ends_of(first, second):
    row = lax.broadcasted_iota(jnp.int32, (8, first.shape[1]), 0)
    parts = [jnp.broadcast_to(v, row.shape) for v in (first, second)]
    (a, b), (c, d) = [[p.astype(jnp.float32) for p in split(v)] for v in parts]
    return row, a, b, c, d


def final_kernel(
    members, z_ref, y_ref, coef_ref,
    a_ref, s_ref, edge_ref, strips_ref, static_ref, turned_ref, strip_ref,
):
    _, levels, cx, cy = a_ref.shape
    along = lax.broadcasted_iota(jnp.int32, (1, cy), 1).astype(jnp.float32)
    for l in range(levels):
        rate = coef_ref[0, l : l + 1, :]
        tall = coef_ref[2, l : l + 1, :]
        ahead = tall * (jnp.exp((along + 1.0) * rate) - jnp.exp((2.0 * cy + 1.0 - along) * rate))
        behind = jnp.exp((cy - along) * rate)
        row, a, b, c, d = ends_of(ahead, behind)
        across = jnp.where(row < 2, a, jnp.where(row == 2, b, jnp.where(row < 5, c, d)))
        row, a, b, c, d = ends_of(y_ref[0, l : l + 1, :], y_ref[1, l : l + 1, :])
        down = jnp.where(row % 3 == 1, jnp.where(row < 3, b, d), jnp.where(row < 3, a, c))
        down = jnp.where(row < 6, down, 0.0)
        field = z_ref[l] + lax.dot_general(
            down.astype(jnp.bfloat16),
            across.astype(jnp.bfloat16),
            (((0,), (0,)), ((), ())),
            preferred_element_type=jnp.float32,
        )
        static_ref[l] = field[:cx]
        for m in range(members):
            a_ref[m, l] = field[(m + 1) * cx : (m + 2) * cx]
    turn(
        static_ref, s_ref, edge_ref, strips_ref, turned_ref, strip_ref, 0, pl.program_id(0)
    )


def transport_kernel(
    s_ref, ut_ref, vt_ref, srow_ref, sstrip_ref, wrow_ref, wstrip_ref, o_ref,
    side_ref, lead_ref, s_buf, u_buf, v_buf,
):
    cx, levels, cy = s_ref.shape
    total = cx + 2 * HALO
    group = pl.program_id(0)
    width = cy // pl.num_programs(0)
    lane = lax.broadcasted_iota(jnp.int32, (levels, cy), 1)
    part = lax.rem(lane, width)
    quarter = width // 4

    def along_x(before, here, after, wind):
        return here + jnp.abs(wind) * (jnp.where(wind > 0.0, before, after) - here)

    def along_y(before, here, after, wind):
        return here + jnp.abs(wind) * (jnp.where(wind > 0.0, before, after) - here)

    @pl.when(group == 0)
    def _():
        def place(x, _):
            for j, (ref, w) in enumerate(((sstrip_ref, 0), (wstrip_ref, 0), (wstrip_ref, 1))):
                left, own, right = [ref[k, w, x].astype(jnp.float32) for k in range(3)]
                far = pltpu.roll(jnp.where(part < quarter, own, right), 2 * quarter, 1)
                side_ref[j, x] = jnp.where(
                    part < quarter, left, jnp.where(part < 2 * quarter, own, far)
                )
            return 0

        lax.fori_loop(0, total, place, 0)
        for p in range(HALO):
            before = side_ref[0, p]
            for x in range(p + 1, total - 1 - p):
                here = side_ref[0, x]
                value = along_x(before, here, side_ref[0, x + 1], side_ref[1, x])
                before = here
                lead_ref[p, x] = jnp.where(
                    part == quarter - 2, pltpu.roll(value, cy - 2 * quarter - 2, 1), value
                )
                side_ref[0, x] = along_y(
                    pltpu.roll(value, 1, 1), value, pltpu.roll(value, cy - 1, 1), side_ref[2, x]
                )

    for buf, center, row_ref, w in (
        (s_buf, s_ref, srow_ref, 0), (u_buf, ut_ref, wrow_ref, 0), (v_buf, vt_ref, wrow_ref, 1)
    ):
        buf[:HALO] = row_ref[0, w].astype(jnp.float32)
        buf[HALO : HALO + cx] = center[...].astype(jnp.float32)
        buf[HALO + cx :] = row_ref[1, w].astype(jnp.float32)
    shift = cy - (group * width + quarter - 1)
    for p in range(HALO):
        before = s_buf[p]
        for x in range(p + 1, total - 1 - p):
            here = s_buf[x]
            value = along_x(before, here, s_buf[x + 1], u_buf[x])
            before = here
            lead = pltpu.roll(lead_ref[p, x], shift, 1)
            value = along_y(
                jnp.where(lane == 0, lead, pltpu.roll(value, 1, 1)),
                value,
                jnp.where(lane == cy - 1, lead, pltpu.roll(value, cy - 1, 1)),
                v_buf[x],
            )
            if p < HALO - 1:
                s_buf[x] = value
            else:
                o_ref[pl.ds(x - HALO, levels, stride=cx), :] = value


def body(
    increment,
    ensemble,
    wind_u,
    wind_v,
    filter_length,
    jacobian,
    obs_weight,
    departure,
    obs_home,
    obs_line,
    obs_count,
):
    axes = ("gx", "gy")
    home_count = lax.axis_size(axes)
    records_here = obs_home.shape[0]
    most = (records_here + home_count - 1) // home_count
    lev, cx, cy = increment.shape
    members = ensemble.shape[0]
    fields = members + 1
    slot_count = home_count * most
    index = jnp.arange(records_here, dtype=jnp.int32)
    earlier = (obs_home[:, None] == obs_home[None, :]) & (index[None, :] < index[:, None])
    slot_of = obs_home * most + jnp.sum(earlier.astype(jnp.int32), axis=1)
    placing = slot_of[:, None] == jnp.arange(slot_count, dtype=jnp.int32)[None, :]
    order, lines, counts = [
        jnp.sum(jnp.where(placing, value[:, None], 0), axis=0)
        for value in (index, obs_line, obs_count)
    ]
    got, note = observe(
        order, lines, counts, jacobian[0], obs_weight, departure, axes, most, 3
    )
    across = jnp.transpose(increment, (1, 0, 2))
    rate = -1.0 / filter_length
    tall = -1.0 / jnp.expm1(2.0 * rate)
    gain = -jnp.expm1(rate) * jnp.sqrt(-jnp.expm1(2.0 * rate))
    coef = jnp.broadcast_to(jnp.stack([rate, gain, tall])[:, :, None], (3, lev, cy))
    size_x, size_y = lax.axis_size("gx"), lax.axis_size("gy")
    part = lev // size_x
    tile = 8
    steps = lev // tile
    pieces = tile // part

    def levels_first(*shape):
        return pl.BlockSpec((tile,) + shape, lambda i: (i, 0, 0))

    def levels_second(*shape):
        first, *rest = shape
        return pl.BlockSpec((first, tile) + tuple(rest), lambda i: (0, i) + (0,) * len(rest))

    def whole(array):
        return pl.BlockSpec(
            array.shape, lambda i: (0,) * array.ndim, pipeline_mode=pl.Buffered(1)
        )

    params = pltpu.CompilerParams(
        dimension_semantics=("arbitrary",), vmem_limit_bytes=56 * 1024 * 1024
    )
    rows = fields * cx
    local, state_x, turned_u, turned_v, wind_edge, wind_strip = pl.pallas_call(
        functools.partial(fields_kernel, members, most),
        grid=(steps,),
        in_specs=[
            pl.BlockSpec(memory_space=pltpu.SMEM),
            whole(got),
            whole(across),
            levels_second(members, cx, cy),
            levels_second(3, cy),
            levels_first(cx, cy),
            levels_first(cx, cy),
        ],
        out_specs=[
            pl.BlockSpec((tile * rows, cy), lambda i: (i, 0)),
            pl.BlockSpec((pieces, 2 * fields, part, cy), lambda i: (i, 0, 0, 0)),
            levels_second(cx, cy),
            levels_second(cx, cy),
            pl.BlockSpec((2, 2, HALO, tile, cy), lambda i: (0, 0, 0, i, 0)),
            pl.BlockSpec((2, cx, tile, cy), lambda i: (0, 0, 0, 0)),
        ],
        out_shape=[
            jax.ShapeDtypeStruct((lev * rows, cy), jnp.float32),
            jax.ShapeDtypeStruct((size_x, 2 * fields, part, cy), jnp.bfloat16),
            jax.ShapeDtypeStruct((cx, lev, cy), jnp.bfloat16),
            jax.ShapeDtypeStruct((cx, lev, cy), jnp.bfloat16),
            jax.ShapeDtypeStruct((2, 2, HALO, lev, cy), jnp.bfloat16),
            jax.ShapeDtypeStruct((2, cx, tile, cy), jnp.bfloat16),
        ],
        scratch_shapes=[
            pltpu.VMEM((cx * lev, cy), jnp.float32),
            pltpu.VMEM((members * tile * cx, cy), jnp.float32),
            pltpu.VMEM((rows, tile, cy), jnp.float32),
            pltpu.VMEM((cx * tile, cy), jnp.float32),
            pltpu.VMEM((2, cx * tile, cy), jnp.float32),
        ],
        compiler_params=params,
        name="fields",
    )(note, got, across, ensemble, coef, wind_u, wind_v)
    local = local.reshape(lev, rows, cy)

    vmem = pl.BlockSpec(memory_space=pltpu.VMEM)
    split_coef = jnp.moveaxis(coef.reshape(3, size_x, part, cy), 1, 0)
    swept = pl.pallas_call(
        functools.partial(carry_x_kernel, cx),
        out_shape=jax.ShapeDtypeStruct((2 * fields, lev, cy), jnp.float32),
        in_specs=[vmem, vmem],
        out_specs=vmem,
        scratch_shapes=[pltpu.VMEM(state_x.shape, jnp.bfloat16)] * 3
        + [pltpu.SemaphoreType.DMA((4, size_x))],
        compiler_params=pltpu.CompilerParams(collective_id=1, has_side_effects=True),
        name="carry_x",
    )(state_x, split_coef)

    z, state_y = pl.pallas_call(
        functools.partial(rows_kernel, fields),
        grid=(steps,),
        in_specs=[levels_first(rows, cy), levels_second(2 * fields, cy), levels_second(3, cy)],
        out_specs=[levels_first(rows, cy), levels_second(2, rows)],
        out_shape=[
            jax.ShapeDtypeStruct((lev, rows, cy), jnp.float32),
            jax.ShapeDtypeStruct((2, lev, rows), jnp.bfloat16),
        ],
        scratch_shapes=[
            pltpu.VMEM((2, tile, rows), jnp.float32),
            pltpu.VMEM((cy, cy), jnp.float32),
            pltpu.VMEM((cy, cy), jnp.float32),
        ],
        compiler_params=params,
        name="rows",
    )(local, swept, coef)

    entered, wind_rows, wind_strips = pl.pallas_call(
        functools.partial(carry_y_kernel, cy),
        out_shape=[jax.ShapeDtypeStruct((2, lev, rows), jnp.float32)]
        + edge_shapes(2, lev, cx, cy),
        in_specs=[vmem] * 4,
        out_specs=[vmem] * 3,
        scratch_shapes=[
            pltpu.VMEM((size_y, 2, lev, rows), jnp.bfloat16),
            pltpu.SemaphoreType.DMA((2, size_y)),
            pltpu.SemaphoreType.DMA((2, 2, 8)),
        ],
        compiler_params=pltpu.CompilerParams(collective_id=2, has_side_effects=True),
        name="carry_y",
    )(state_y, coef, wind_edge, wind_strip)

    grad_alpha, static, edge, strip = pl.pallas_call(
        functools.partial(final_kernel, members),
        grid=(steps,),
        in_specs=[levels_first(rows, cy), levels_second(2, rows), levels_second(3, cy)],
        out_specs=[
            levels_second(members, cx, cy),
            levels_second(cx, cy),
            pl.BlockSpec((2, 1, HALO, tile, cy), lambda i: (0, 0, 0, i, 0)),
            pl.BlockSpec((1, cx, tile, cy), lambda i: (0, 0, 0, 0)),
        ],
        out_shape=[
            jax.ShapeDtypeStruct((members, lev, cx, cy), jnp.float32),
            jax.ShapeDtypeStruct((cx, lev, cy), jnp.float32),
            jax.ShapeDtypeStruct((2, 1, HALO, lev, cy), jnp.bfloat16),
            jax.ShapeDtypeStruct((1, cx, tile, cy), jnp.bfloat16),
        ],
        scratch_shapes=[
            pltpu.VMEM((tile, cx, cy), jnp.float32),
            pltpu.VMEM((cx * tile, cy), jnp.float32),
            pltpu.VMEM((1, cx * tile, cy), jnp.float32),
        ],
        compiler_params=params,
        name="final",
    )(z, entered, coef)

    edge_rows, edge_strips = pl.pallas_call(
        halo_kernel,
        out_shape=edge_shapes(1, lev, cx, cy),
        in_specs=[vmem] * 2,
        out_specs=[vmem] * 2,
        scratch_shapes=[pltpu.SemaphoreType.DMA((2, 2, 8))],
        compiler_params=pltpu.CompilerParams(collective_id=5, has_side_effects=True),
        name="halo",
    )(edge, strip)

    def rows_of(array):
        return pl.BlockSpec(array.shape[:3] + (tile, cy), lambda i: (0, 0, 0, i, 0))

    extent = cx + 2 * HALO
    static = pl.pallas_call(
        transport_kernel,
        grid=(steps,),
        in_specs=[
            levels_second(cx, cy),
            levels_second(cx, cy),
            levels_second(cx, cy),
            rows_of(edge_rows),
            whole(edge_strips),
            rows_of(wind_rows),
            whole(wind_strips),
        ],
        out_specs=pl.BlockSpec((tile * cx, cy), lambda i: (i, 0)),
        out_shape=jax.ShapeDtypeStruct((lev * cx, cy), jnp.float32),
        scratch_shapes=[
            pltpu.VMEM((3, extent, tile, cy), jnp.float32),
            pltpu.VMEM((HALO, extent, tile, cy), jnp.float32),
            pltpu.VMEM((extent, tile, cy), jnp.float32),
            pltpu.VMEM((extent, tile, cy), jnp.float32),
            pltpu.VMEM((extent, tile, cy), jnp.float32),
        ],
        compiler_params=params,
        name="transport",
    )(static, turned_u, turned_v, edge_rows, edge_strips, wind_rows, wind_strips)
    static = static.reshape(lev, cx, cy)
    return (grad_alpha, static)


def solution(mesh):
    return jax.shard_map(
        body,
        mesh=mesh,
        in_specs=(
            P(None, "gx", "gy"),
            P(None, None, "gx", "gy"),
            P(None, "gx", "gy"),
            P(None, "gx", "gy"),
            P(),
            P(("gx", "gy"), None, None),
            P(("gx", "gy"), None),
            P(("gx", "gy"), None, None),
            P(("gx", "gy")),
            P(("gx", "gy")),
            P(("gx", "gy")),
        ),
        out_specs=(P(None, None, "gx", "gy"), P(None, "gx", "gy")),
        check_vma=False,
    )
```

```python
import functools
import jax
import jax.numpy as jnp
from jax import lax
from jax.experimental import pallas as pl
from jax.experimental.pallas import tpu as pltpu
from jax.sharding import PartitionSpec as P

HALO = 3
CODE = 32767.0
highest = lax.Precision.HIGHEST


def peer_id(axes, index):
    if len(axes) == 1:
        return {axes[0]: index}
    minor = lax.axis_size(axes[1])
    return {axes[0]: index // minor, axes[1]: index % minor}


def split(value):
    high = value.astype(jnp.bfloat16)
    return high, (value - high.astype(jnp.float32)).astype(jnp.bfloat16)


def position(axes):
    me = lax.axis_index(axes[0])
    for name in axes[1:]:
        me = me * lax.axis_size(name) + lax.axis_index(name)
    return me


def coded(value):
    top = jnp.max(jnp.max(jnp.abs(value), axis=1, keepdims=True), axis=0, keepdims=True)
    top = jnp.maximum(top, 1e-30)
    code = jnp.round(value * (CODE / top)).astype(jnp.int32).astype(jnp.int16)
    return code, top * (1.0 / CODE)


def obs_kernel(
    axes, most, order_ref, line_ref, count_ref, j_ref, w_ref, d_hbm, got_ref, note_ref,
    d_buf, send_buf, note_buf, lhs_ref, hold_ref, scale_ref,
    d_sem, send_sem, recv_sem, note_send, note_recv,
):
    count = lax.axis_size(axes)
    half = count // 2
    me = position(axes)
    lev = j_ref.shape[1]
    cy = d_buf.shape[2]
    barrier = pltpu.get_barrier_semaphore()
    pieces = d_sem.shape[0]
    size = d_buf.shape[0] // pieces

    def piece(i):
        rows = pl.ds(i * size, size)
        return pltpu.make_async_copy(d_hbm.at[rows], d_buf.at[rows], d_sem.at[i])

    for i in range(pieces):
        piece(i).start()

    def greet(k, _):
        pl.semaphore_signal(
            barrier,
            inc=1,
            device_id=peer_id(axes, lax.rem(me + k, count)),
            device_id_type=pl.DeviceIdType.MESH,
        )
        return 0

    lax.fori_loop(1, count, greet, 0)
    turned = j_ref[...].astype(jnp.float32).T
    high, low = split(turned * w_ref[...])
    lhs_ref[...] = jnp.concatenate([high, low], axis=0)
    both = jnp.dot(lhs_ref[...], j_ref[...], preferred_element_type=jnp.float32)
    normal = both[:lev] + both[lev:]
    code, scale = coded(normal)
    hold_ref[...] = jnp.concatenate([code[: lev // 2], code[lev // 2 :]], axis=1)
    scale_ref[...] = jnp.broadcast_to(scale, scale_ref.shape)
    for i in range(pieces):
        piece(i).wait()
    pl.semaphore_wait(barrier, count - 1)
    lane = lax.broadcasted_iota(jnp.int32, (1, cy), 1)

    def fill(home, target, note):
        blocks = [d_buf[order_ref[home * most + m]] for m in range(most)]
        both = jnp.dot(
            lhs_ref[...], jnp.concatenate(blocks, axis=1), preferred_element_type=jnp.float32
        )
        word = jnp.where(lane == 3 * most, scale_ref[0:1, :], 0.0)
        for m in range(most):
            part = both[:lev, m * cy : (m + 1) * cy] + both[lev:, m * cy : (m + 1) * cy]
            code, scale = coded(part)
            target[m * lev : (m + 1) * lev, :] = code
            word = jnp.where(lane == m, line_ref[home * most + m].astype(jnp.float32), word)
            word = jnp.where(lane == most + m, count_ref[home * most + m].astype(jnp.float32), word)
            word = jnp.where(lane == 2 * most + m, scale, word)
        target[most * lev :, :] = hold_ref[...]
        note[...] = word

    def goal(t):
        j = t + t // half
        mine, place = me // half, lax.rem(me, half)
        other = lax.rem(mine + 1 + j // half, 2)
        return other * half + lax.rem(place + j, half)

    def sends(to, origin):
        peer = dict(device_id=peer_id(axes, to), device_id_type=pl.DeviceIdType.MESH)
        return (
            pltpu.make_async_remote_copy(
                src_ref=send_buf.at[to], dst_ref=got_ref.at[origin],
                send_sem=send_sem.at[to], recv_sem=recv_sem.at[origin], **peer
            ),
            pltpu.make_async_remote_copy(
                src_ref=note_buf.at[to], dst_ref=note_ref.at[origin],
                send_sem=note_send.at[to], recv_sem=note_recv.at[origin], **peer
            ),
        )

    def begin(to):
        for copy in sends(to, me):
            copy.start()

    first = goal(0)
    fill(first, send_buf.at[first], note_buf.at[first])

    def step(t, _):
        to = goal(t)
        fill(to, send_buf.at[to], note_buf.at[to])
        begin(goal(t - 1))
        return 0

    lax.fori_loop(1, count - 1, step, 0)
    fill(me, got_ref.at[me], note_ref.at[me])
    begin(goal(count - 2))

    def finish(k, _):
        peer = lax.rem(me + k, count)
        for copy in sends(peer, peer):
            copy.wait_send()
            copy.wait_recv()
        return 0

    lax.fori_loop(1, count, finish, 0)


def observe(order, lines, counts, jacobian, weight, departure, axes, most, collective_id):
    count = lax.axis_size(axes)
    channels, lev = jacobian.shape
    records, _, cy = departure.shape
    rows = most * lev + lev // 2
    smem = pl.BlockSpec(memory_space=pltpu.SMEM)
    vmem = pl.BlockSpec(memory_space=pltpu.VMEM)
    dma = pltpu.SemaphoreType.DMA
    return pl.pallas_call(
        functools.partial(obs_kernel, axes, most),
        out_shape=[
            pltpu.VMEM((count, rows, cy), jnp.int16),
            pltpu.VMEM((count, 1, cy), jnp.float32),
        ],
        in_specs=[smem, smem, smem, vmem, vmem, pl.BlockSpec(memory_space=pltpu.HBM)],
        out_specs=[vmem, vmem],
        scratch_shapes=[
            pltpu.VMEM((records, channels, cy), jnp.bfloat16),
            pltpu.VMEM((count, rows, cy), jnp.int16),
            pltpu.VMEM((count, 1, cy), jnp.float32),
            pltpu.VMEM((2 * lev, channels), jnp.bfloat16),
            pltpu.VMEM((lev // 2, 2 * lev), jnp.int16),
            pltpu.VMEM((8, cy), jnp.float32),
            dma((8,)), dma((count,)), dma((count,)), dma((count,)), dma((count,)),
        ],
        compiler_params=pltpu.CompilerParams(
            collective_id=collective_id,
            has_side_effects=True,
            vmem_limit_bytes=24 * 1024 * 1024,
        ),
        name="observe",
    )(order, lines, counts, jacobian, weight, pltpu.with_memory_space_constraint(departure, pltpu.HBM))


def home_sums(most, note_ref, got_ref, c_ref, sum_ref):
    homes = got_ref.shape[0]
    lev, cy = c_ref.shape[1:]
    sum_ref[...] = jnp.zeros(sum_ref.shape, sum_ref.dtype)
    lane = lax.broadcasted_iota(jnp.int32, (lev // 2, 2 * lev), 1)
    column = lax.broadcasted_iota(jnp.int32, (lev, cy), 1)

    def one(k, _):
        code = got_ref[k, most * lev :, :].astype(jnp.int32).astype(jnp.float32)
        high, low = split(code)
        high, low = high.astype(jnp.float32), low.astype(jnp.float32)
        matrix = jnp.concatenate(
            [
                jnp.where(lane < lev, high, pltpu.roll(low, lev, 1)),
                jnp.where(lane < lev, pltpu.roll(high, lev, 1), low),
            ],
            axis=0,
        ).astype(jnp.bfloat16)
        lines = [note_ref[k, 0, m].astype(jnp.int32) for m in range(most)]
        block = jnp.concatenate([c_ref[line] for line in lines], axis=1)
        product = jnp.dot(
            matrix, jnp.concatenate([block, block], axis=0), preferred_element_type=jnp.float32
        )
        for m in range(most):
            part = got_ref[k, m * lev : (m + 1) * lev, :].astype(jnp.int32).astype(jnp.float32)
            value = (
                note_ref[k, 0, 3 * most] * product[:, m * cy : (m + 1) * cy]
                - note_ref[k, 0, 2 * most + m] * part
            )
            value = jnp.where(column < note_ref[k, 0, most + m].astype(jnp.int32), value, 0.0)
            rows = pl.ds(pl.multiple_of(lines[m] * lev, lev), lev)
            sum_ref[rows, :] += value
        return 0

    lax.fori_loop(0, homes, one, 0)


def ways():
    return [(dx, dy) for dx in (-1, 0, 1) for dy in (-1, 0, 1) if (dx, dy) != (0, 0)]


class Edges:
    def __init__(self, edge_ref, strip_ref, rows_ref, strips_ref, sems):
        self.refs = edge_ref, strip_ref, rows_ref, strips_ref
        self.sems = sems
        self.at = lax.axis_index("gx"), lax.axis_index("gy")
        self.size = lax.axis_size("gx"), lax.axis_size("gy")

    def present(self, dx, dy):
        x, y = self.at[0] + dx, self.at[1] + dy
        return (x >= 0) & (x < self.size[0]) & (y >= 0) & (y < self.size[1])

    def copies(self, k, dx, dy):
        edge_ref, strip_ref, rows_ref, strips_ref = self.refs
        cx = strip_ref.shape[1]
        slot = 1 - dy
        if dx == 0:
            pairs = [(strip_ref, strips_ref.at[slot, :, pl.ds(HALO, cx)])]
        else:
            first = cx - HALO if dx == 1 else 0
            target = 0 if dx == 1 else cx + HALO
            pairs = [
                (
                    strip_ref.at[:, pl.ds(first, HALO)],
                    strips_ref.at[slot, :, pl.ds(target, HALO)],
                )
            ]
            if dy == 0:
                side = 0 if dx == 1 else 1
                pairs.append((edge_ref.at[1 - side], rows_ref.at[side]))
        return [
            pltpu.make_async_remote_copy(
                src_ref=source,
                dst_ref=target,
                send_sem=self.sems.at[0, j, k],
                recv_sem=self.sems.at[1, j, k],
                device_id={"gx": self.at[0] + dx, "gy": self.at[1] + dy},
                device_id_type=pl.DeviceIdType.MESH,
            )
            for j, (source, target) in enumerate(pairs)
        ]

    def greet(self, barrier):
        around = 0
        for dx, dy in ways():
            here = self.present(dx, dy)
            around = around + here.astype(jnp.int32)

            @pl.when(here)
            def _():
                pl.semaphore_signal(
                    barrier,
                    inc=1,
                    device_id={"gx": self.at[0] + dx, "gy": self.at[1] + dy},
                    device_id_type=pl.DeviceIdType.MESH,
                )

        return around

    def send(self):
        _, strip_ref, rows_ref, strips_ref = self.refs
        for k, (dx, dy) in enumerate(ways()):

            @pl.when(self.present(dx, dy))
            def _():
                for copy in self.copies(k, dx, dy):
                    copy.start()

        cx = strip_ref.shape[1]
        strips_ref[1, :, HALO : HALO + cx] = strip_ref[...]
        for dx, dy in ways():
            rows = HALO if dx else cx
            first = HALO if dx == 0 else 0 if dx == 1 else cx + HALO

            @pl.when(jnp.logical_not(self.present(-dx, -dy)))
            def _():
                blank = strips_ref[1 - dy, :, first : first + rows]
                strips_ref[1 - dy, :, first : first + rows] = jnp.zeros(blank.shape, blank.dtype)
                if dy == 0:
                    side = 0 if dx == 1 else 1
                    rows_ref[side] = jnp.zeros(rows_ref.shape[1:], rows_ref.dtype)

    def finish(self):
        for k, (dx, dy) in enumerate(ways()):

            @pl.when(self.present(dx, dy))
            def _():
                for copy in self.copies(k, dx, dy):
                    copy.wait_send()

            @pl.when(self.present(-dx, -dy))
            def _():
                for copy in self.copies(k, dx, dy):
                    copy.wait_recv()


def edge_shapes(arrays, lev, cx, cy):
    return [
        pltpu.VMEM((2, arrays, HALO, lev, cy), jnp.bfloat16),
        pltpu.VMEM((3, arrays, cx + 2 * HALO, 8, cy), jnp.bfloat16),
    ]


def halo_kernel(edge_ref, strip_ref, rows_ref, strips_ref, sems):
    edges = Edges(edge_ref, strip_ref, rows_ref, strips_ref, sems)
    barrier = pltpu.get_barrier_semaphore()
    around = edges.greet(barrier)
    pl.semaphore_wait(barrier, around)
    edges.send()
    edges.finish()


def put_strip(turned_ref, strip_ref, w, group):
    width = turned_ref.shape[1] // pl.num_programs(0)
    value = turned_ref[...]
    lane = lax.broadcasted_iota(jnp.int32, value.shape, 1)
    first = group * width
    moved = pltpu.roll(value, first + width // 4, 1)
    here = (lane >= first) & (lane < first + width // 2)
    strip_ref[w] = jnp.where(here, moved, strip_ref[w])


def turn(value_ref, out_ref, edge_ref, strips_ref, turned_ref, strip_ref, w, group):
    levels, cx, cy = value_ref.shape
    for l in range(levels):
        turned_ref[pl.ds(l, cx, stride=levels), :] = value_ref[l].astype(jnp.float32)
    turned = turned_ref[...].reshape(cx, levels, cy)
    out_ref[...] = turned.astype(out_ref.dtype)
    edge_ref[0, w] = turned[:HALO].astype(edge_ref.dtype)
    edge_ref[1, w] = turned[cx - HALO :].astype(edge_ref.dtype)

    @pl.when(group == 0)
    def _():
        strip_ref[w] = jnp.zeros(strip_ref.shape[1:], strip_ref.dtype)

    put_strip(turned_ref, strip_ref, w, group)

    @pl.when(group == pl.num_programs(0) - 1)
    def _():
        strips_ref[w] = strip_ref[w].reshape(cx, levels, cy).astype(strips_ref.dtype)


def fields_kernel(
    members, most, note_ref, got_ref, c_ref, e_ref, coef_ref, u_ref, v_ref,
    x_ref, state_ref, ut_ref, vt_ref, edge_ref, strips_ref,
    sum_ref, ens_ref, run_ref, turned_ref, strip_ref,
):
    _, levels, cx, cy = e_ref.shape
    lev = c_ref.shape[1]
    fields = members + 1
    pieces, _, part, _ = state_ref.shape
    i = pl.program_id(0)

    @pl.when(i == 0)
    def _():
        home_sums(most, note_ref, got_ref, c_ref, sum_ref)

    for w, (wind_ref, wt_ref) in enumerate(((u_ref, ut_ref), (v_ref, vt_ref))):
        turn(wind_ref, wt_ref, edge_ref, strips_ref, turned_ref, strip_ref, w, i)
    for m in range(members):
        for l in range(levels):
            start = (m * levels + l) * cx
            ens_ref[start : start + cx, :] = e_ref[m, l].astype(jnp.float32)
    decay = jnp.exp(coef_ref[0])
    scale = coef_ref[1]
    state = [jnp.zeros((levels, cy), jnp.float32)] * fields
    for x in range(cx):
        base = sum_ref[pl.ds(x * lev + i * levels, levels), :] * scale
        for k in range(fields):
            value = base
            if k:
                value = base * ens_ref[pl.ds((k - 1) * levels * cx + x, levels, stride=cx), :]
            state[k] = value + decay * state[k]
            run_ref[k * cx + x] = state[k]
    for j in range(pieces):
        for k in range(fields):
            state_ref[j, k] = state[k][j * part : (j + 1) * part].astype(state_ref.dtype)
    state = [jnp.zeros((levels, cy), jnp.float32)] * fields
    for x in reversed(range(cx)):
        for k in range(fields):
            state[k] = run_ref[k * cx + x] + decay * state[k]
            first = i * levels * fields * cx + k * cx + x
            x_ref[pl.ds(first, levels, stride=fields * cx), :] = state[k]
    for j in range(pieces):
        for k in range(fields):
            state_ref[j, fields + k] = state[k][j * part : (j + 1) * part].astype(state_ref.dtype)


def carry_x_kernel(cells, s_ref, coef_ref, o_ref, in_ref, mid_ref, out_ref, sems):
    size = lax.axis_size("gx")
    me = lax.axis_index("gx")
    fields = s_ref.shape[1] // 2
    barrier = pltpu.get_barrier_semaphore()

    def greet(k, _):
        pl.semaphore_signal(
            barrier,
            inc=1,
            device_id={"gx": lax.rem(me + k, size)},
            device_id_type=pl.DeviceIdType.MESH,
        )
        return 0

    lax.fori_loop(1, size, greet, 0)
    in_ref[me] = s_ref[me]
    pl.semaphore_wait(barrier, size - 1)

    def copy(source, target, first, to, slot):
        return pltpu.make_async_remote_copy(
            src_ref=source.at[to],
            dst_ref=target.at[slot],
            send_sem=sems.at[first, to],
            recv_sem=sems.at[first + 1, slot],
            device_id={"gx": to},
            device_id_type=pl.DeviceIdType.MESH,
        )

    def swap(source, target, first):
        def send(k, _):
            copy(source, target, first, lax.rem(me + k, size), me).start()
            return 0

        def finish(k, _):
            peer = lax.rem(me + k, size)
            landed = copy(source, target, first, peer, peer)
            landed.wait_send()
            landed.wait_recv()
            return 0

        lax.fori_loop(1, size, send, 0)
        lax.fori_loop(1, size, finish, 0)

    swap(s_ref, in_ref, 0)
    rate = coef_ref[me, 0]
    step = jnp.exp(rate * cells)
    link = coef_ref[me, 2] * (jnp.exp(rate) - jnp.exp(rate * (2 * cells + 1)))
    for k in range(fields):
        enter = jnp.zeros(rate.shape, jnp.float32)
        entered = []
        for t in range(size):
            entered.append(enter)
            mid_ref[t, k] = enter.astype(mid_ref.dtype)
            enter = in_ref[t, k].astype(jnp.float32) + step * enter
        leave = jnp.zeros(rate.shape, jnp.float32)
        for t in reversed(range(size)):
            mid_ref[t, fields + k] = leave.astype(mid_ref.dtype)
            leave = in_ref[t, fields + k].astype(jnp.float32) + link * entered[t] + step * leave
    out_ref[me] = mid_ref[me]
    swap(mid_ref, out_ref, 2)
    parts, part = out_ref.shape[0], out_ref.shape[2]
    for t in range(parts):
        for k in range(2 * fields):
            o_ref[k, t * part : (t + 1) * part, :] = out_ref[t, k].astype(jnp.float32)


def rows_kernel(fields, x_ref, enter_ref, coef_ref, z_ref, state_ref, rows_ref, far_ref, sum_ref):
    _, levels, _ = rows_ref.shape
    _, cx, cy = z_ref.shape
    cx = cx // fields
    start = pl.program_id(0) * levels
    along = lax.broadcasted_iota(jnp.int32, (cx, cy), 0).astype(jnp.float32)

    @pl.when(pl.program_id(0) == 0)
    def _():
        row = lax.broadcasted_iota(jnp.int32, (cy, cy), 0)
        col = lax.broadcasted_iota(jnp.int32, (cy, cy), 1)
        far_ref[...] = jnp.abs(row - col).astype(jnp.float32)
        sum_ref[...] = (2 * cy - row - col).astype(jnp.float32)

    row = lax.broadcasted_iota(jnp.int32, (8, cy), 0)
    col = lax.broadcasted_iota(jnp.int32, (8, cy), 1)
    picks = (col == jnp.where(row == 0, cy - 1, jnp.where(row == 1, 0, -1))).astype(jnp.bfloat16)
    for l in range(levels):
        rate = coef_ref[0, l : l + 1, :]
        tall = coef_ref[2, l : l + 1, :]
        ahead = tall * (jnp.exp((along + 1.0) * rate) - jnp.exp((2.0 * cx + 1.0 - along) * rate))
        behind = jnp.exp((cx - along) * rate)
        parts = []
        for k in range(fields):
            parts.append(
                x_ref[start + l, k * cx : (k + 1) * cx, :]
                + ahead * enter_ref[k, l : l + 1, :]
                + behind * enter_ref[fields + k, l : l + 1, :]
            )
        high, low = split(jnp.concatenate(parts, axis=0))
        smooth = (
            coef_ref[1, l : l + 1, :]
            * tall
            * (jnp.exp(far_ref[...] * rate) - jnp.exp(sum_ref[...] * rate))
        )
        m_high, m_low = split(smooth)
        weights = jnp.concatenate(
            [
                jnp.concatenate([m_high, m_low], axis=1),
                jnp.concatenate([m_high, jnp.zeros_like(m_low)], axis=1),
            ],
            axis=0,
        )
        both = jnp.dot(
            jnp.concatenate([high, low], axis=1), weights, preferred_element_type=jnp.float32
        )
        z = both[:, :cy] + both[:, cy:]
        z_ref[start + l] = z
        ends = lax.dot_general(
            picks,
            z.astype(jnp.bfloat16),
            (((1,), (1,)), ((), ())),
            preferred_element_type=jnp.float32,
        )
        rows_ref[0, l : l + 1, :] = ends[0:1]
        rows_ref[1, l : l + 1, :] = ends[1:2]
    state_ref[...] = rows_ref[...].astype(state_ref.dtype)


def carry_y_kernel(
    cells, s_ref, coef_ref, edge_ref, strip_ref, o_ref, rows_ref, strips_ref, in_ref, sems, more
):
    edges = Edges(edge_ref, strip_ref, rows_ref, strips_ref, more)
    size = lax.axis_size("gy")
    me = lax.axis_index("gy")
    _, lev, width = s_ref.shape
    barrier = pltpu.get_barrier_semaphore()
    for k in range(1, size):
        pl.semaphore_signal(
            barrier,
            inc=1,
            device_id={"gy": lax.rem(me + k, size)},
            device_id_type=pl.DeviceIdType.MESH,
        )
    around = edges.greet(barrier)
    in_ref[me] = s_ref[...]
    pl.semaphore_wait(barrier, size - 1 + around)

    def copy(to, slot):
        return pltpu.make_async_remote_copy(
            src_ref=s_ref,
            dst_ref=in_ref.at[slot],
            send_sem=sems.at[0, to],
            recv_sem=sems.at[1, slot],
            device_id={"gy": to},
            device_id_type=pl.DeviceIdType.MESH,
        )

    for k in range(1, size):
        copy(lax.rem(me + k, size), me).start()
    edges.send()
    for k in range(1, size):
        peer = lax.rem(me + k, size)
        landed = copy(peer, peer)
        landed.wait_send()
        landed.wait_recv()
    rate = coef_ref[0, :, 0:1]
    step = jnp.broadcast_to(jnp.exp(rate * cells), (lev, width))
    link = coef_ref[2, :, 0:1] * (jnp.exp(rate) - jnp.exp(rate * (2 * cells + 1)))
    link = jnp.broadcast_to(link, (lev, width))
    enter = jnp.zeros((lev, width), jnp.float32)
    mine = enter
    entered = []
    for t in range(size):
        entered.append(enter)
        mine = jnp.where(me == t, enter, mine)
        enter = in_ref[t, 0].astype(jnp.float32) + step * enter
    leave = jnp.zeros((lev, width), jnp.float32)
    last = leave
    for t in reversed(range(size)):
        last = jnp.where(me == t, leave, last)
        leave = in_ref[t, 1].astype(jnp.float32) + link * entered[t] + step * leave
    o_ref[0] = mine
    o_ref[1] = last
    edges.finish()


def ends_of(first, second):
    row = lax.broadcasted_iota(jnp.int32, (8, first.shape[1]), 0)
    parts = [jnp.broadcast_to(v, row.shape) for v in (first, second)]
    (a, b), (c, d) = [[p.astype(jnp.float32) for p in split(v)] for v in parts]
    return row, a, b, c, d


def final_kernel(
    members, z_ref, y_ref, coef_ref,
    a_ref, s_ref, edge_ref, strips_ref, static_ref, turned_ref, strip_ref,
):
    _, levels, cx, cy = a_ref.shape
    along = lax.broadcasted_iota(jnp.int32, (1, cy), 1).astype(jnp.float32)
    for l in range(levels):
        rate = coef_ref[0, l : l + 1, :]
        tall = coef_ref[2, l : l + 1, :]
        ahead = tall * (jnp.exp((along + 1.0) * rate) - jnp.exp((2.0 * cy + 1.0 - along) * rate))
        behind = jnp.exp((cy - along) * rate)
        row, a, b, c, d = ends_of(ahead, behind)
        across = jnp.where(row < 2, a, jnp.where(row == 2, b, jnp.where(row < 5, c, d)))
        row, a, b, c, d = ends_of(y_ref[0, l : l + 1, :], y_ref[1, l : l + 1, :])
        down = jnp.where(row % 3 == 1, jnp.where(row < 3, b, d), jnp.where(row < 3, a, c))
        down = jnp.where(row < 6, down, 0.0)
        field = z_ref[pl.program_id(0) * levels + l] + lax.dot_general(
            down.astype(jnp.bfloat16),
            across.astype(jnp.bfloat16),
            (((0,), (0,)), ((), ())),
            preferred_element_type=jnp.float32,
        )
        static_ref[l] = field[:cx]
        for m in range(members):
            a_ref[m, l] = field[(m + 1) * cx : (m + 2) * cx]
    turn(
        static_ref, s_ref, edge_ref, strips_ref, turned_ref, strip_ref, 0, pl.program_id(0)
    )


def transport_kernel(
    s_ref, ut_ref, vt_ref, srow_ref, sstrip_ref, wrow_ref, wstrip_ref, o_ref,
    side_ref, lead_ref, s_buf, u_buf, v_buf,
):
    cx, levels, cy = s_ref.shape
    total = cx + 2 * HALO
    group = pl.program_id(0)
    width = cy // pl.num_programs(0)
    lane = lax.broadcasted_iota(jnp.int32, (levels, cy), 1)
    part = lax.rem(lane, width)
    quarter = width // 4

    def along_x(before, here, after, wind):
        return here + jnp.abs(wind) * (jnp.where(wind > 0.0, before, after) - here)

    def along_y(before, here, after, wind):
        return here + jnp.abs(wind) * (jnp.where(wind > 0.0, before, after) - here)

    @pl.when(group == 0)
    def _():
        def place(x, _):
            for j, (ref, w) in enumerate(((sstrip_ref, 0), (wstrip_ref, 0), (wstrip_ref, 1))):
                left, own, right = [ref[k, w, x].astype(jnp.float32) for k in range(3)]
                far = pltpu.roll(jnp.where(part < quarter, own, right), 2 * quarter, 1)
                side_ref[j, x] = jnp.where(
                    part < quarter, left, jnp.where(part < 2 * quarter, own, far)
                )
            return 0

        lax.fori_loop(0, total, place, 0)
        for p in range(HALO):
            before = side_ref[0, p]
            for x in range(p + 1, total - 1 - p):
                here = side_ref[0, x]
                value = along_x(before, here, side_ref[0, x + 1], side_ref[1, x])
                before = here
                lead_ref[p, x] = jnp.where(
                    part == quarter - 2, pltpu.roll(value, cy - 2 * quarter - 2, 1), value
                )
                side_ref[0, x] = along_y(
                    pltpu.roll(value, 1, 1), value, pltpu.roll(value, cy - 1, 1), side_ref[2, x]
                )

    for buf, center, row_ref, w in (
        (s_buf, s_ref, srow_ref, 0), (u_buf, ut_ref, wrow_ref, 0), (v_buf, vt_ref, wrow_ref, 1)
    ):
        buf[:HALO] = row_ref[0, w].astype(jnp.float32)
        buf[HALO : HALO + cx] = center[...].astype(jnp.float32)
        buf[HALO + cx :] = row_ref[1, w].astype(jnp.float32)
    shift = cy - (group * width + quarter - 1)
    for p in range(HALO):
        before = s_buf[p]
        for x in range(p + 1, total - 1 - p):
            here = s_buf[x]
            value = along_x(before, here, s_buf[x + 1], u_buf[x])
            before = here
            lead = pltpu.roll(lead_ref[p, x], shift, 1)
            value = along_y(
                jnp.where(lane == 0, lead, pltpu.roll(value, 1, 1)),
                value,
                jnp.where(lane == cy - 1, lead, pltpu.roll(value, cy - 1, 1)),
                v_buf[x],
            )
            if p < HALO - 1:
                s_buf[x] = value
            else:
                o_ref[pl.ds(x - HALO, levels, stride=cx), :] = value


def body(
    increment,
    ensemble,
    wind_u,
    wind_v,
    filter_length,
    jacobian,
    obs_weight,
    departure,
    obs_home,
    obs_line,
    obs_count,
):
    axes = ("gx", "gy")
    home_count = lax.axis_size(axes)
    records_here = obs_home.shape[0]
    most = (records_here + home_count - 1) // home_count
    lev, cx, cy = increment.shape
    members = ensemble.shape[0]
    fields = members + 1
    slot_count = home_count * most
    index = jnp.arange(records_here, dtype=jnp.int32)
    earlier = (obs_home[:, None] == obs_home[None, :]) & (index[None, :] < index[:, None])
    slot_of = obs_home * most + jnp.sum(earlier.astype(jnp.int32), axis=1)
    placing = slot_of[:, None] == jnp.arange(slot_count, dtype=jnp.int32)[None, :]
    order, lines, counts = [
        jnp.sum(jnp.where(placing, value[:, None], 0), axis=0)
        for value in (index, obs_line, obs_count)
    ]
    got, note = observe(
        order, lines, counts, jacobian[0], obs_weight, departure, axes, most, 3
    )
    across = jnp.transpose(increment, (1, 0, 2))
    rate = -1.0 / filter_length
    tall = -1.0 / jnp.expm1(2.0 * rate)
    gain = -jnp.expm1(rate) * jnp.sqrt(-jnp.expm1(2.0 * rate))
    coef = jnp.broadcast_to(jnp.stack([rate, gain, tall])[:, :, None], (3, lev, cy))
    size_x, size_y = lax.axis_size("gx"), lax.axis_size("gy")
    part = lev // size_x
    tile = 8
    steps = lev // tile
    pieces = tile // part

    def levels_first(*shape):
        return pl.BlockSpec((tile,) + shape, lambda i: (i, 0, 0))

    def levels_second(*shape):
        first, *rest = shape
        return pl.BlockSpec((first, tile) + tuple(rest), lambda i: (0, i) + (0,) * len(rest))

    def whole(array):
        return pl.BlockSpec(
            array.shape, lambda i: (0,) * array.ndim, pipeline_mode=pl.Buffered(1)
        )

    params = pltpu.CompilerParams(
        dimension_semantics=("arbitrary",), vmem_limit_bytes=32 * 1024 * 1024
    )
    rows = fields * cx
    vmem = pl.BlockSpec(memory_space=pltpu.VMEM)
    local, state_x, turned_u, turned_v, wind_edge, wind_strip = pl.pallas_call(
        functools.partial(fields_kernel, members, most),
        grid=(steps,),
        in_specs=[
            pl.BlockSpec(memory_space=pltpu.SMEM),
            whole(got),
            whole(across),
            levels_second(members, cx, cy),
            levels_second(3, cy),
            levels_first(cx, cy),
            levels_first(cx, cy),
        ],
        out_specs=[
            vmem,
            pl.BlockSpec((pieces, 2 * fields, part, cy), lambda i: (i, 0, 0, 0)),
            levels_second(cx, cy),
            levels_second(cx, cy),
            pl.BlockSpec((2, 2, HALO, tile, cy), lambda i: (0, 0, 0, i, 0)),
            pl.BlockSpec((2, cx, tile, cy), lambda i: (0, 0, 0, 0)),
        ],
        out_shape=[
            pltpu.VMEM((lev * rows, cy), jnp.float32),
            pltpu.VMEM((size_x, 2 * fields, part, cy), jnp.bfloat16),
            pltpu.VMEM((cx, lev, cy), jnp.bfloat16),
            pltpu.VMEM((cx, lev, cy), jnp.bfloat16),
            pltpu.VMEM((2, 2, HALO, lev, cy), jnp.bfloat16),
            pltpu.VMEM((2, cx, tile, cy), jnp.bfloat16),
        ],
        scratch_shapes=[
            pltpu.VMEM((cx * lev, cy), jnp.float32),
            pltpu.VMEM((members * tile * cx, cy), jnp.float32),
            pltpu.VMEM((rows, tile, cy), jnp.float32),
            pltpu.VMEM((cx * tile, cy), jnp.float32),
            pltpu.VMEM((2, cx * tile, cy), jnp.float32),
        ],
        compiler_params=params,
        name="fields",
    )(note, got, across, ensemble, coef, wind_u, wind_v)
    local = local.reshape(lev, rows, cy)

    split_coef = jnp.moveaxis(coef.reshape(3, size_x, part, cy), 1, 0)
    swept = pl.pallas_call(
        functools.partial(carry_x_kernel, cx),
        out_shape=pltpu.VMEM((2 * fields, lev, cy), jnp.float32),
        in_specs=[vmem, vmem],
        out_specs=vmem,
        scratch_shapes=[pltpu.VMEM(state_x.shape, jnp.bfloat16)] * 3
        + [pltpu.SemaphoreType.DMA((4, size_x))],
        compiler_params=pltpu.CompilerParams(
            collective_id=1, has_side_effects=True, vmem_limit_bytes=12 * 1024 * 1024
        ),
        name="carry_x",
    )(state_x, split_coef)

    z, state_y = pl.pallas_call(
        functools.partial(rows_kernel, fields),
        grid=(steps,),
        in_specs=[vmem, levels_second(2 * fields, cy), levels_second(3, cy)],
        out_specs=[vmem, levels_second(2, rows)],
        out_shape=[
            pltpu.VMEM((lev, rows, cy), jnp.float32),
            pltpu.VMEM((2, lev, rows), jnp.bfloat16),
        ],
        scratch_shapes=[
            pltpu.VMEM((2, tile, rows), jnp.float32),
            pltpu.VMEM((cy, cy), jnp.float32),
            pltpu.VMEM((cy, cy), jnp.float32),
        ],
        compiler_params=params,
        name="rows",
    )(local, swept, coef)

    entered, wind_rows, wind_strips = pl.pallas_call(
        functools.partial(carry_y_kernel, cy),
        out_shape=[pltpu.VMEM((2, lev, rows), jnp.float32)]
        + edge_shapes(2, lev, cx, cy),
        in_specs=[vmem] * 4,
        out_specs=[vmem] * 3,
        scratch_shapes=[
            pltpu.VMEM((size_y, 2, lev, rows), jnp.bfloat16),
            pltpu.SemaphoreType.DMA((2, size_y)),
            pltpu.SemaphoreType.DMA((2, 2, 8)),
        ],
        compiler_params=pltpu.CompilerParams(
            collective_id=2, has_side_effects=True, vmem_limit_bytes=12 * 1024 * 1024
        ),
        name="carry_y",
    )(state_y, coef, wind_edge, wind_strip)

    grad_alpha, static, edge, strip = pl.pallas_call(
        functools.partial(final_kernel, members),
        grid=(steps,),
        in_specs=[vmem, levels_second(2, rows), levels_second(3, cy)],
        out_specs=[
            levels_second(members, cx, cy),
            levels_second(cx, cy),
            pl.BlockSpec((2, 1, HALO, tile, cy), lambda i: (0, 0, 0, i, 0)),
            pl.BlockSpec((1, cx, tile, cy), lambda i: (0, 0, 0, 0)),
        ],
        out_shape=[
            jax.ShapeDtypeStruct((members, lev, cx, cy), jnp.float32),
            pltpu.VMEM((cx, lev, cy), jnp.float32),
            pltpu.VMEM((2, 1, HALO, lev, cy), jnp.bfloat16),
            pltpu.VMEM((1, cx, tile, cy), jnp.bfloat16),
        ],
        scratch_shapes=[
            pltpu.VMEM((tile, cx, cy), jnp.float32),
            pltpu.VMEM((cx * tile, cy), jnp.float32),
            pltpu.VMEM((1, cx * tile, cy), jnp.float32),
        ],
        compiler_params=params,
        name="final",
    )(z, entered, coef)

    edge_rows, edge_strips = pl.pallas_call(
        halo_kernel,
        out_shape=edge_shapes(1, lev, cx, cy),
        in_specs=[vmem] * 2,
        out_specs=[vmem] * 2,
        scratch_shapes=[pltpu.SemaphoreType.DMA((2, 2, 8))],
        compiler_params=pltpu.CompilerParams(
            collective_id=5, has_side_effects=True, vmem_limit_bytes=12 * 1024 * 1024
        ),
        name="halo",
    )(edge, strip)

    def rows_of(array):
        return pl.BlockSpec(array.shape[:3] + (tile, cy), lambda i: (0, 0, 0, i, 0))

    extent = cx + 2 * HALO
    static = pl.pallas_call(
        transport_kernel,
        grid=(steps,),
        in_specs=[
            levels_second(cx, cy),
            levels_second(cx, cy),
            levels_second(cx, cy),
            rows_of(edge_rows),
            whole(edge_strips),
            rows_of(wind_rows),
            whole(wind_strips),
        ],
        out_specs=pl.BlockSpec((tile * cx, cy), lambda i: (i, 0)),
        out_shape=jax.ShapeDtypeStruct((lev * cx, cy), jnp.float32),
        scratch_shapes=[
            pltpu.VMEM((3, extent, tile, cy), jnp.float32),
            pltpu.VMEM((HALO, extent, tile, cy), jnp.float32),
            pltpu.VMEM((extent, tile, cy), jnp.float32),
            pltpu.VMEM((extent, tile, cy), jnp.float32),
            pltpu.VMEM((extent, tile, cy), jnp.float32),
        ],
        compiler_params=params,
        name="transport",
    )(static, turned_u, turned_v, edge_rows, edge_strips, wind_rows, wind_strips)
    static = static.reshape(lev, cx, cy)
    return (grad_alpha, static)


def solution(mesh):
    return jax.shard_map(
        body,
        mesh=mesh,
        in_specs=(
            P(None, "gx", "gy"),
            P(None, None, "gx", "gy"),
            P(None, "gx", "gy"),
            P(None, "gx", "gy"),
            P(),
            P(("gx", "gy"), None, None),
            P(("gx", "gy"), None),
            P(("gx", "gy"), None, None),
            P(("gx", "gy")),
            P(("gx", "gy")),
            P(("gx", "gy")),
        ),
        out_specs=(P(None, None, "gx", "gy"), P(None, "gx", "gy")),
        check_vma=False,
    )
```

```python
import functools
import jax
import jax.numpy as jnp
from jax import lax
from jax.experimental import pallas as pl
from jax.experimental.pallas import tpu as pltpu
from jax.sharding import PartitionSpec as P

HALO = 3
CODE = 32767.0
highest = lax.Precision.HIGHEST


def peer_id(axes, index):
    if len(axes) == 1:
        return {axes[0]: index}
    minor = lax.axis_size(axes[1])
    return {axes[0]: index // minor, axes[1]: index % minor}


def split(value):
    high = value.astype(jnp.bfloat16)
    return high, (value - high.astype(jnp.float32)).astype(jnp.bfloat16)


def position(axes):
    me = lax.axis_index(axes[0])
    for name in axes[1:]:
        me = me * lax.axis_size(name) + lax.axis_index(name)
    return me


def coded(value):
    top = jnp.max(jnp.max(jnp.abs(value), axis=1, keepdims=True), axis=0, keepdims=True)
    top = jnp.maximum(top, 1e-30)
    code = jnp.round(value * (CODE / top)).astype(jnp.int32).astype(jnp.int16)
    return code, top * (1.0 / CODE)


def obs_kernel(
    axes, most, order_ref, line_ref, count_ref, j_ref, w_ref, d_hbm, c_ref, sum_ref, note_ref,
    d_buf, send_buf, got_ref, scale_buf, scale_ref, note_buf, note_smem, lhs_ref, hold_ref,
    gram_ref, gain_ref, d_sem, sems, gram_sem, smem_sem,
):
    count = lax.axis_size(axes)
    size_x, size_y = lax.axis_size("gx"), lax.axis_size("gy")
    at_x, at_y = lax.axis_index("gx"), lax.axis_index("gy")
    half = count // 2
    me = position(axes)
    lev = j_ref.shape[1]
    cy = d_buf.shape[2]
    mesh_id = pl.DeviceIdType.MESH
    barrier = pltpu.get_barrier_semaphore()
    pieces = d_sem.shape[0]
    size = d_buf.shape[0] // pieces

    def piece(i):
        rows = pl.ds(i * size, size)
        return pltpu.make_async_copy(d_hbm.at[rows], d_buf.at[rows], d_sem.at[i])

    for i in range(pieces):
        piece(i).start()

    def greet(k, _):
        pl.semaphore_signal(
            barrier,
            inc=1,
            device_id=peer_id(axes, lax.rem(me + k, count)),
            device_id_type=mesh_id,
        )
        return 0

    lax.fori_loop(1, count, greet, 0)
    lane = lax.broadcasted_iota(jnp.int32, (1, cy), 1)

    def words(home, _):
        word = jnp.zeros((1, cy), jnp.int32)
        for m in range(most):
            word = jnp.where(lane == m, line_ref[home * most + m], word)
            word = jnp.where(lane == most + m, count_ref[home * most + m], word)
        note_buf[home] = word
        return 0

    lax.fori_loop(0, count, words, 0)
    turned = j_ref[...].astype(jnp.float32).T
    high, low = split(turned * w_ref[...])
    lhs_ref[...] = jnp.concatenate([high, low], axis=0)
    both = jnp.dot(lhs_ref[...], j_ref[...], preferred_element_type=jnp.float32)
    normal = both[:lev] + both[lev:]
    code, gain = coded(normal)
    hold_ref[...] = jnp.concatenate([code[: lev // 2], code[lev // 2 :]], axis=1)
    gain_ref[...] = jnp.broadcast_to(gain, gain_ref.shape)
    gram_ref[at_y, at_x] = hold_ref[...]
    note_ref[me] = note_buf[me]
    pl.semaphore_wait(barrier, count - 1)

    def remote(kind, source, target, to, slot):
        return pltpu.make_async_remote_copy(
            src_ref=source,
            dst_ref=target,
            send_sem=sems.at[kind, to],
            recv_sem=sems.at[kind + 1, slot],
            device_id=peer_id(axes, to),
            device_id_type=mesh_id,
        )

    def notes(to, slot):
        return remote(4, note_buf.at[to], note_ref.at[slot], to, slot)

    def gram_x(to, slot):
        return pltpu.make_async_remote_copy(
            src_ref=hold_ref,
            dst_ref=gram_ref.at[at_y, slot],
            send_sem=gram_sem.at[0, to],
            recv_sem=gram_sem.at[1, slot],
            device_id={"gx": to},
            device_id_type=mesh_id,
        )

    def gram_y(to, slot):
        return pltpu.make_async_remote_copy(
            src_ref=gram_ref.at[at_y],
            dst_ref=gram_ref.at[slot],
            send_sem=gram_sem.at[2, to],
            recv_sem=gram_sem.at[3, slot],
            device_id={"gy": to},
            device_id_type=mesh_id,
        )

    def early(k, _):
        gram_x(lax.rem(at_x + k, size_x), at_x).start()
        return 0

    def tell(k, _):
        notes(lax.rem(me + k, count), me).start()
        return 0

    lax.fori_loop(1, size_x, early, 0)
    lax.fori_loop(1, count, tell, 0)
    for i in range(pieces):
        piece(i).wait()

    def fill(home, target, scale_row):
        blocks = [d_buf[order_ref[home * most + m]] for m in range(most)]
        both = jnp.dot(
            lhs_ref[...], jnp.concatenate(blocks, axis=1), preferred_element_type=jnp.float32
        )
        word = gain_ref[0:1, :]
        for m in range(most):
            part = both[:lev, m * cy : (m + 1) * cy] + both[lev:, m * cy : (m + 1) * cy]
            code, scale = coded(part)
            target[m * lev : (m + 1) * lev, :] = code
            word = jnp.where(lane == m, scale, word)
        scale_row[...] = word

    def goal(t):
        j = t + t // half
        mine, place = me // half, lax.rem(me, half)
        other = lax.rem(mine + 1 + j // half, 2)
        return other * half + lax.rem(place + j, half)

    def sends(to, origin):
        return (
            remote(0, send_buf.at[to], got_ref.at[origin], to, origin),
            remote(2, scale_buf.at[to], scale_ref.at[origin], to, origin),
        )

    def begin(to):
        for copy in sends(to, me):
            copy.start()

    first = goal(0)
    fill(first, send_buf.at[first], scale_buf.at[first])
    fill(me, got_ref.at[me], scale_ref.at[me])
    begin(first)

    def step(t, _):
        pair = [goal(2 * t + 1 + k) for k in range(2)]
        for to in pair:
            fill(to, send_buf.at[to], scale_buf.at[to])
        for to in pair:
            begin(to)
        return 0

    lax.fori_loop(0, half - 1, step, 0)

    def landed_x(k, _):
        peer = lax.rem(at_x + k, size_x)
        gram_x(peer, peer).wait_send()
        gram_x(peer, peer).wait_recv()
        return 0

    lax.fori_loop(1, size_x, landed_x, 0)
    for k in range(1, size_y):
        gram_y(lax.rem(at_y + k, size_y), at_y).start()

    def told(k, _):
        peer = lax.rem(me + k, count)
        notes(peer, peer).wait_send()
        notes(peer, peer).wait_recv()
        return 0

    lax.fori_loop(1, count, told, 0)
    to_smem = pltpu.make_async_copy(note_ref, note_smem, smem_sem)
    to_smem.start()
    to_smem.wait()
    wide = lax.broadcasted_iota(jnp.int32, (lev // 2, 2 * lev), 1)

    def product(at, k):
        code = at.astype(jnp.int32).astype(jnp.float32)
        high, low = split(code)
        high, low = high.astype(jnp.float32), low.astype(jnp.float32)
        matrix = jnp.concatenate(
            [
                jnp.where(wide < lev, high, pltpu.roll(low, lev, 1)),
                jnp.where(wide < lev, pltpu.roll(high, lev, 1), low),
            ],
            axis=0,
        ).astype(jnp.bfloat16)
        block = jnp.concatenate([c_ref[note_smem[k, 0, m]] for m in range(most)], axis=1)
        both = jnp.dot(
            matrix, jnp.concatenate([block, block], axis=0), preferred_element_type=jnp.float32
        )
        for m in range(most):
            sum_ref[k * most + m] = both[:, m * cy : (m + 1) * cy]

    def products(y):
        def four(x, _):
            for k in range(4):
                product(gram_ref[y, 4 * x + k], (4 * x + k) * size_y + y)
            return 0

        lax.fori_loop(0, size_x // 4, four, 0)

    products(at_y)
    for k in range(1, size_y):
        peer = lax.rem(at_y + k, size_y)
        gram_y(peer, peer).wait_send()
        gram_y(peer, peer).wait_recv()
        products(peer)
    column = lax.broadcasted_iota(jnp.int32, (lev, cy), 1)

    def settle(k):
        scales = scale_ref[k]
        for m in range(most):
            part = got_ref[k, m * lev : (m + 1) * lev, :].astype(jnp.int32).astype(jnp.float32)
            value = scales[:, most : most + 1] * sum_ref[k * most + m] - scales[:, m : m + 1] * part
            sum_ref[k * most + m] = jnp.where(column < note_smem[k, 0, most + m], value, 0.0)

    def wait(peer):
        for copy in sends(peer, peer):
            copy.wait_send()
            copy.wait_recv()

    wait(first)
    settle(me)
    settle(first)

    def finish(t, _):
        pair = [goal(2 * t + 1 + k) for k in range(2)]
        for peer in pair:
            wait(peer)
        for peer in pair:
            settle(peer)
        return 0

    lax.fori_loop(0, half - 1, finish, 0)


def observe(order, lines, counts, jacobian, weight, departure, across, axes, most, collective_id):
    count = lax.axis_size(axes)
    size_x, size_y = lax.axis_size("gx"), lax.axis_size("gy")
    channels, lev = jacobian.shape
    records, _, cy = departure.shape
    smem = pl.BlockSpec(memory_space=pltpu.SMEM)
    vmem = pl.BlockSpec(memory_space=pltpu.VMEM)
    dma = pltpu.SemaphoreType.DMA
    return pl.pallas_call(
        functools.partial(obs_kernel, axes, most),
        out_shape=[
            pltpu.VMEM((count * most, lev, cy), jnp.float32),
            pltpu.VMEM((count, 1, cy), jnp.int32),
        ],
        in_specs=[smem, smem, smem, vmem, vmem, pl.BlockSpec(memory_space=pltpu.HBM), vmem],
        out_specs=[vmem, vmem],
        scratch_shapes=[
            pltpu.VMEM((records, channels, cy), jnp.bfloat16),
            pltpu.VMEM((count, most * lev, cy), jnp.int16),
            pltpu.VMEM((count, most * lev, cy), jnp.int16),
            pltpu.VMEM((count, 1, cy), jnp.float32),
            pltpu.VMEM((count, 1, cy), jnp.float32),
            pltpu.VMEM((count, 1, cy), jnp.int32),
            pltpu.SMEM((count, 1, cy), jnp.int32),
            pltpu.VMEM((2 * lev, channels), jnp.bfloat16),
            pltpu.VMEM((lev // 2, 2 * lev), jnp.int16),
            pltpu.VMEM((size_y, size_x, lev // 2, 2 * lev), jnp.int16),
            pltpu.VMEM((8, cy), jnp.float32),
            dma((8,)), dma((6, count)), dma((4, max(size_x, size_y))), dma,
        ],
        compiler_params=pltpu.CompilerParams(
            collective_id=collective_id,
            has_side_effects=True,
            vmem_limit_bytes=28 * 1024 * 1024,
        ),
        name="observe",
    )(
        order, lines, counts, jacobian, weight,
        pltpu.with_memory_space_constraint(departure, pltpu.HBM), across,
    )


def home_sums(most, note_ref, got_ref, sum_ref):
    slots, lev, _ = got_ref.shape
    sum_ref[...] = jnp.zeros(sum_ref.shape, sum_ref.dtype)

    def one(k, _):
        for m in range(most):
            rows = pl.ds(pl.multiple_of(note_ref[k, 0, m] * lev, lev), lev)
            sum_ref[rows, :] += got_ref[k * most + m]
        return 0

    lax.fori_loop(0, slots // most, one, 0)


def ways():
    return [(dx, dy) for dx in (-1, 0, 1) for dy in (-1, 0, 1) if (dx, dy) != (0, 0)]


class Edges:
    def __init__(self, edge_ref, strip_ref, rows_ref, strips_ref, sems):
        self.refs = edge_ref, strip_ref, rows_ref, strips_ref
        self.sems = sems
        self.at = lax.axis_index("gx"), lax.axis_index("gy")
        self.size = lax.axis_size("gx"), lax.axis_size("gy")

    def present(self, dx, dy):
        x, y = self.at[0] + dx, self.at[1] + dy
        return (x >= 0) & (x < self.size[0]) & (y >= 0) & (y < self.size[1])

    def copies(self, k, dx, dy):
        edge_ref, strip_ref, rows_ref, strips_ref = self.refs
        cx = strip_ref.shape[1]
        slot = 1 - dy
        if dx == 0:
            pairs = [(strip_ref, strips_ref.at[slot, :, pl.ds(HALO, cx)])]
        else:
            first = cx - HALO if dx == 1 else 0
            target = 0 if dx == 1 else cx + HALO
            pairs = [
                (
                    strip_ref.at[:, pl.ds(first, HALO)],
                    strips_ref.at[slot, :, pl.ds(target, HALO)],
                )
            ]
            if dy == 0:
                side = 0 if dx == 1 else 1
                pairs.append((edge_ref.at[1 - side], rows_ref.at[side]))
        return [
            pltpu.make_async_remote_copy(
                src_ref=source,
                dst_ref=target,
                send_sem=self.sems.at[0, j, k],
                recv_sem=self.sems.at[1, j, k],
                device_id={"gx": self.at[0] + dx, "gy": self.at[1] + dy},
                device_id_type=pl.DeviceIdType.MESH,
            )
            for j, (source, target) in enumerate(pairs)
        ]

    def greet(self, barrier):
        around = 0
        for dx, dy in ways():
            here = self.present(dx, dy)
            around = around + here.astype(jnp.int32)

            @pl.when(here)
            def _():
                pl.semaphore_signal(
                    barrier,
                    inc=1,
                    device_id={"gx": self.at[0] + dx, "gy": self.at[1] + dy},
                    device_id_type=pl.DeviceIdType.MESH,
                )

        return around

    def send(self):
        _, strip_ref, rows_ref, strips_ref = self.refs
        for k, (dx, dy) in enumerate(ways()):

            @pl.when(self.present(dx, dy))
            def _():
                for copy in self.copies(k, dx, dy):
                    copy.start()

        cx = strip_ref.shape[1]
        strips_ref[1, :, HALO : HALO + cx] = strip_ref[...]
        for dx, dy in ways():
            rows = HALO if dx else cx
            first = HALO if dx == 0 else 0 if dx == 1 else cx + HALO

            @pl.when(jnp.logical_not(self.present(-dx, -dy)))
            def _():
                blank = strips_ref[1 - dy, :, first : first + rows]
                strips_ref[1 - dy, :, first : first + rows] = jnp.zeros(blank.shape, blank.dtype)
                if dy == 0:
                    side = 0 if dx == 1 else 1
                    rows_ref[side] = jnp.zeros(rows_ref.shape[1:], rows_ref.dtype)

    def finish(self):
        for k, (dx, dy) in enumerate(ways()):

            @pl.when(self.present(dx, dy))
            def _():
                for copy in self.copies(k, dx, dy):
                    copy.wait_send()

            @pl.when(self.present(-dx, -dy))
            def _():
                for copy in self.copies(k, dx, dy):
                    copy.wait_recv()


def edge_shapes(arrays, lev, cx, cy):
    return [
        pltpu.VMEM((2, arrays, HALO, lev, cy), jnp.bfloat16),
        pltpu.VMEM((3, arrays, cx + 2 * HALO, 8, cy), jnp.bfloat16),
    ]


def halo_kernel(edge_ref, strip_ref, rows_ref, strips_ref, sems):
    edges = Edges(edge_ref, strip_ref, rows_ref, strips_ref, sems)
    barrier = pltpu.get_barrier_semaphore()
    around = edges.greet(barrier)
    pl.semaphore_wait(barrier, around)
    edges.send()
    edges.finish()


def put_strip(turned_ref, strip_ref, w, group):
    width = turned_ref.shape[1] // pl.num_programs(0)
    value = turned_ref[...]
    lane = lax.broadcasted_iota(jnp.int32, value.shape, 1)
    first = group * width
    moved = pltpu.roll(value, first + width // 4, 1)
    here = (lane >= first) & (lane < first + width // 2)
    strip_ref[w] = jnp.where(here, moved, strip_ref[w])


def turn(value_ref, out_ref, edge_ref, strips_ref, turned_ref, strip_ref, w, group):
    levels, cx, cy = value_ref.shape
    for l in range(levels):
        turned_ref[pl.ds(l, cx, stride=levels), :] = value_ref[l].astype(jnp.float32)
    turned = turned_ref[...].reshape(cx, levels, cy)
    out_ref[...] = turned.astype(out_ref.dtype)
    edge_ref[0, w] = turned[:HALO].astype(edge_ref.dtype)
    edge_ref[1, w] = turned[cx - HALO :].astype(edge_ref.dtype)

    @pl.when(group == 0)
    def _():
        strip_ref[w] = jnp.zeros(strip_ref.shape[1:], strip_ref.dtype)

    put_strip(turned_ref, strip_ref, w, group)

    @pl.when(group == pl.num_programs(0) - 1)
    def _():
        strips_ref[w] = strip_ref[w].reshape(cx, levels, cy).astype(strips_ref.dtype)


def fields_kernel(
    members, most, note_ref, got_ref, e_ref, coef_ref, u_ref, v_ref,
    x_ref, state_ref, ut_ref, vt_ref, edge_ref, strips_ref,
    sum_ref, ens_ref, run_ref, turned_ref, strip_ref,
):
    _, levels, cx, cy = e_ref.shape
    lev = got_ref.shape[1]
    fields = members + 1
    pieces, _, part, _ = state_ref.shape
    i = pl.program_id(0)

    @pl.when(i == 0)
    def _():
        home_sums(most, note_ref, got_ref, sum_ref)

    for w, (wind_ref, wt_ref) in enumerate(((u_ref, ut_ref), (v_ref, vt_ref))):
        turn(wind_ref, wt_ref, edge_ref, strips_ref, turned_ref, strip_ref, w, i)
    for m in range(members):
        for l in range(levels):
            start = (m * levels + l) * cx
            ens_ref[start : start + cx, :] = e_ref[m, l].astype(jnp.float32)
    decay = jnp.exp(coef_ref[0])
    scale = coef_ref[1]
    state = [jnp.zeros((levels, cy), jnp.float32)] * fields
    for x in range(cx):
        base = sum_ref[pl.ds(x * lev + i * levels, levels), :] * scale
        for k in range(fields):
            value = base
            if k:
                value = base * ens_ref[pl.ds((k - 1) * levels * cx + x, levels, stride=cx), :]
            state[k] = value + decay * state[k]
            run_ref[k * cx + x] = state[k]
    for j in range(pieces):
        for k in range(fields):
            state_ref[j, k] = state[k][j * part : (j + 1) * part].astype(state_ref.dtype)
    state = [jnp.zeros((levels, cy), jnp.float32)] * fields
    for x in reversed(range(cx)):
        for k in range(fields):
            state[k] = run_ref[k * cx + x] + decay * state[k]
            first = i * levels * fields * cx + k * cx + x
            x_ref[pl.ds(first, levels, stride=fields * cx), :] = state[k]
    for j in range(pieces):
        for k in range(fields):
            state_ref[j, fields + k] = state[k][j * part : (j + 1) * part].astype(state_ref.dtype)


def carry_x_kernel(cells, s_ref, coef_ref, o_ref, in_ref, mid_ref, out_ref, sems):
    size = lax.axis_size("gx")
    me = lax.axis_index("gx")
    fields = s_ref.shape[1] // 2
    barrier = pltpu.get_barrier_semaphore()

    def greet(k, _):
        pl.semaphore_signal(
            barrier,
            inc=1,
            device_id={"gx": lax.rem(me + k, size)},
            device_id_type=pl.DeviceIdType.MESH,
        )
        return 0

    lax.fori_loop(1, size, greet, 0)
    in_ref[me] = s_ref[me]
    pl.semaphore_wait(barrier, size - 1)

    def copy(source, target, first, to, slot):
        return pltpu.make_async_remote_copy(
            src_ref=source.at[to],
            dst_ref=target.at[slot],
            send_sem=sems.at[first, to],
            recv_sem=sems.at[first + 1, slot],
            device_id={"gx": to},
            device_id_type=pl.DeviceIdType.MESH,
        )

    def swap(source, target, first):
        def send(k, _):
            copy(source, target, first, lax.rem(me + k, size), me).start()
            return 0

        def finish(k, _):
            peer = lax.rem(me + k, size)
            landed = copy(source, target, first, peer, peer)
            landed.wait_send()
            landed.wait_recv()
            return 0

        lax.fori_loop(1, size, send, 0)
        lax.fori_loop(1, size, finish, 0)

    swap(s_ref, in_ref, 0)
    rate = coef_ref[me, 0]
    step = jnp.exp(rate * cells)
    link = coef_ref[me, 2] * (jnp.exp(rate) - jnp.exp(rate * (2 * cells + 1)))
    for k in range(fields):
        enter = jnp.zeros(rate.shape, jnp.float32)
        entered = []
        for t in range(size):
            entered.append(enter)
            mid_ref[t, k] = enter.astype(mid_ref.dtype)
            enter = in_ref[t, k].astype(jnp.float32) + step * enter
        leave = jnp.zeros(rate.shape, jnp.float32)
        for t in reversed(range(size)):
            mid_ref[t, fields + k] = leave.astype(mid_ref.dtype)
            leave = in_ref[t, fields + k].astype(jnp.float32) + link * entered[t] + step * leave
    out_ref[me] = mid_ref[me]
    swap(mid_ref, out_ref, 2)
    parts, part = out_ref.shape[0], out_ref.shape[2]
    for t in range(parts):
        for k in range(2 * fields):
            o_ref[k, t * part : (t + 1) * part, :] = out_ref[t, k].astype(jnp.float32)


def rows_kernel(fields, x_ref, enter_ref, coef_ref, z_ref, state_ref, rows_ref, far_ref, sum_ref):
    _, levels, _ = rows_ref.shape
    _, cx, cy = z_ref.shape
    cx = cx // fields
    start = pl.program_id(0) * levels
    along = lax.broadcasted_iota(jnp.int32, (cx, cy), 0).astype(jnp.float32)

    @pl.when(pl.program_id(0) == 0)
    def _():
        row = lax.broadcasted_iota(jnp.int32, (cy, cy), 0)
        col = lax.broadcasted_iota(jnp.int32, (cy, cy), 1)
        far_ref[...] = jnp.abs(row - col).astype(jnp.float32)
        sum_ref[...] = (2 * cy - row - col).astype(jnp.float32)

    row = lax.broadcasted_iota(jnp.int32, (8, cy), 0)
    col = lax.broadcasted_iota(jnp.int32, (8, cy), 1)
    picks = (col == jnp.where(row == 0, cy - 1, jnp.where(row == 1, 0, -1))).astype(jnp.bfloat16)
    for l in range(levels):
        rate = coef_ref[0, l : l + 1, :]
        tall = coef_ref[2, l : l + 1, :]
        ahead = tall * (jnp.exp((along + 1.0) * rate) - jnp.exp((2.0 * cx + 1.0 - along) * rate))
        behind = jnp.exp((cx - along) * rate)
        parts = []
        for k in range(fields):
            parts.append(
                x_ref[start + l, k * cx : (k + 1) * cx, :]
                + ahead * enter_ref[k, l : l + 1, :]
                + behind * enter_ref[fields + k, l : l + 1, :]
            )
        high, low = split(jnp.concatenate(parts, axis=0))
        smooth = (
            coef_ref[1, l : l + 1, :]
            * tall
            * (jnp.exp(far_ref[...] * rate) - jnp.exp(sum_ref[...] * rate))
        )
        m_high, m_low = split(smooth)
        weights = jnp.concatenate(
            [
                jnp.concatenate([m_high, m_low], axis=1),
                jnp.concatenate([m_high, jnp.zeros_like(m_low)], axis=1),
            ],
            axis=0,
        )
        both = jnp.dot(
            jnp.concatenate([high, low], axis=1), weights, preferred_element_type=jnp.float32
        )
        z = both[:, :cy] + both[:, cy:]
        z_ref[start + l] = z
        ends = lax.dot_general(
            picks,
            z.astype(jnp.bfloat16),
            (((1,), (1,)), ((), ())),
            preferred_element_type=jnp.float32,
        )
        rows_ref[0, l : l + 1, :] = ends[0:1]
        rows_ref[1, l : l + 1, :] = ends[1:2]
    state_ref[...] = rows_ref[...].astype(state_ref.dtype)


def carry_y_kernel(
    cells, s_ref, coef_ref, edge_ref, strip_ref, o_ref, rows_ref, strips_ref, in_ref, sems, more
):
    edges = Edges(edge_ref, strip_ref, rows_ref, strips_ref, more)
    size = lax.axis_size("gy")
    me = lax.axis_index("gy")
    _, lev, width = s_ref.shape
    barrier = pltpu.get_barrier_semaphore()
    for k in range(1, size):
        pl.semaphore_signal(
            barrier,
            inc=1,
            device_id={"gy": lax.rem(me + k, size)},
            device_id_type=pl.DeviceIdType.MESH,
        )
    around = edges.greet(barrier)
    in_ref[me] = s_ref[...]
    pl.semaphore_wait(barrier, size - 1 + around)

    def copy(to, slot):
        return pltpu.make_async_remote_copy(
            src_ref=s_ref,
            dst_ref=in_ref.at[slot],
            send_sem=sems.at[0, to],
            recv_sem=sems.at[1, slot],
            device_id={"gy": to},
            device_id_type=pl.DeviceIdType.MESH,
        )

    for k in range(1, size):
        copy(lax.rem(me + k, size), me).start()
    edges.send()
    for k in range(1, size):
        peer = lax.rem(me + k, size)
        landed = copy(peer, peer)
        landed.wait_send()
        landed.wait_recv()
    rate = coef_ref[0, :, 0:1]
    step = jnp.broadcast_to(jnp.exp(rate * cells), (lev, width))
    link = coef_ref[2, :, 0:1] * (jnp.exp(rate) - jnp.exp(rate * (2 * cells + 1)))
    link = jnp.broadcast_to(link, (lev, width))
    enter = jnp.zeros((lev, width), jnp.float32)
    mine = enter
    entered = []
    for t in range(size):
        entered.append(enter)
        mine = jnp.where(me == t, enter, mine)
        enter = in_ref[t, 0].astype(jnp.float32) + step * enter
    leave = jnp.zeros((lev, width), jnp.float32)
    last = leave
    for t in reversed(range(size)):
        last = jnp.where(me == t, leave, last)
        leave = in_ref[t, 1].astype(jnp.float32) + link * entered[t] + step * leave
    o_ref[0] = mine
    o_ref[1] = last
    edges.finish()


def ends_of(first, second):
    row = lax.broadcasted_iota(jnp.int32, (8, first.shape[1]), 0)
    parts = [jnp.broadcast_to(v, row.shape) for v in (first, second)]
    (a, b), (c, d) = [[p.astype(jnp.float32) for p in split(v)] for v in parts]
    return row, a, b, c, d


def final_kernel(
    members, z_ref, y_ref, coef_ref,
    a_ref, s_ref, edge_ref, strips_ref, static_ref, turned_ref, strip_ref,
):
    _, levels, cx, cy = a_ref.shape
    along = lax.broadcasted_iota(jnp.int32, (1, cy), 1).astype(jnp.float32)
    for l in range(levels):
        rate = coef_ref[0, l : l + 1, :]
        tall = coef_ref[2, l : l + 1, :]
        ahead = tall * (jnp.exp((along + 1.0) * rate) - jnp.exp((2.0 * cy + 1.0 - along) * rate))
        behind = jnp.exp((cy - along) * rate)
        row, a, b, c, d = ends_of(ahead, behind)
        across = jnp.where(row < 2, a, jnp.where(row == 2, b, jnp.where(row < 5, c, d)))
        row, a, b, c, d = ends_of(y_ref[0, l : l + 1, :], y_ref[1, l : l + 1, :])
        down = jnp.where(row % 3 == 1, jnp.where(row < 3, b, d), jnp.where(row < 3, a, c))
        down = jnp.where(row < 6, down, 0.0)
        field = z_ref[pl.program_id(0) * levels + l] + lax.dot_general(
            down.astype(jnp.bfloat16),
            across.astype(jnp.bfloat16),
            (((0,), (0,)), ((), ())),
            preferred_element_type=jnp.float32,
        )
        static_ref[l] = field[:cx]
        for m in range(members):
            a_ref[m, l] = field[(m + 1) * cx : (m + 2) * cx]
    turn(
        static_ref, s_ref, edge_ref, strips_ref, turned_ref, strip_ref, 0, pl.program_id(0)
    )


def transport_kernel(
    s_ref, ut_ref, vt_ref, srow_ref, sstrip_ref, wrow_ref, wstrip_ref, o_ref,
    side_ref, lead_ref, s_buf, u_buf, v_buf,
):
    cx, levels, cy = s_ref.shape
    total = cx + 2 * HALO
    group = pl.program_id(0)
    width = cy // pl.num_programs(0)
    lane = lax.broadcasted_iota(jnp.int32, (levels, cy), 1)
    part = lax.rem(lane, width)
    quarter = width // 4

    def along_x(before, here, after, wind):
        return here + jnp.abs(wind) * (jnp.where(wind > 0.0, before, after) - here)

    def along_y(before, here, after, wind):
        return here + jnp.abs(wind) * (jnp.where(wind > 0.0, before, after) - here)

    @pl.when(group == 0)
    def _():
        def place(x, _):
            for j, (ref, w) in enumerate(((sstrip_ref, 0), (wstrip_ref, 0), (wstrip_ref, 1))):
                left, own, right = [ref[k, w, x].astype(jnp.float32) for k in range(3)]
                far = pltpu.roll(jnp.where(part < quarter, own, right), 2 * quarter, 1)
                side_ref[j, x] = jnp.where(
                    part < quarter, left, jnp.where(part < 2 * quarter, own, far)
                )
            return 0

        lax.fori_loop(0, total, place, 0)
        for p in range(HALO):
            before = side_ref[0, p]
            for x in range(p + 1, total - 1 - p):
                here = side_ref[0, x]
                value = along_x(before, here, side_ref[0, x + 1], side_ref[1, x])
                before = here
                lead_ref[p, x] = jnp.where(
                    part == quarter - 2, pltpu.roll(value, cy - 2 * quarter - 2, 1), value
                )
                side_ref[0, x] = along_y(
                    pltpu.roll(value, 1, 1), value, pltpu.roll(value, cy - 1, 1), side_ref[2, x]
                )

    for buf, center, row_ref, w in (
        (s_buf, s_ref, srow_ref, 0), (u_buf, ut_ref, wrow_ref, 0), (v_buf, vt_ref, wrow_ref, 1)
    ):
        buf[:HALO] = row_ref[0, w].astype(jnp.float32)
        buf[HALO : HALO + cx] = center[...].astype(jnp.float32)
        buf[HALO + cx :] = row_ref[1, w].astype(jnp.float32)
    shift = cy - (group * width + quarter - 1)
    for p in range(HALO):
        before = s_buf[p]
        for x in range(p + 1, total - 1 - p):
            here = s_buf[x]
            value = along_x(before, here, s_buf[x + 1], u_buf[x])
            before = here
            lead = pltpu.roll(lead_ref[p, x], shift, 1)
            value = along_y(
                jnp.where(lane == 0, lead, pltpu.roll(value, 1, 1)),
                value,
                jnp.where(lane == cy - 1, lead, pltpu.roll(value, cy - 1, 1)),
                v_buf[x],
            )
            if p < HALO - 1:
                s_buf[x] = value
            else:
                o_ref[pl.ds(x - HALO, levels, stride=cx), :] = value


def body(
    increment,
    ensemble,
    wind_u,
    wind_v,
    filter_length,
    jacobian,
    obs_weight,
    departure,
    obs_home,
    obs_line,
    obs_count,
):
    axes = ("gx", "gy")
    home_count = lax.axis_size(axes)
    records_here = obs_home.shape[0]
    most = (records_here + home_count - 1) // home_count
    lev, cx, cy = increment.shape
    members = ensemble.shape[0]
    fields = members + 1
    slot_count = home_count * most
    index = jnp.arange(records_here, dtype=jnp.int32)
    earlier = (obs_home[:, None] == obs_home[None, :]) & (index[None, :] < index[:, None])
    slot_of = obs_home * most + jnp.sum(earlier.astype(jnp.int32), axis=1)
    placing = slot_of[:, None] == jnp.arange(slot_count, dtype=jnp.int32)[None, :]
    order, lines, counts = [
        jnp.sum(jnp.where(placing, value[:, None], 0), axis=0)
        for value in (index, obs_line, obs_count)
    ]
    across = jnp.transpose(increment, (1, 0, 2))
    got, note = observe(
        order, lines, counts, jacobian[0], obs_weight, departure, across, axes, most, 3
    )
    rate = -1.0 / filter_length
    tall = -1.0 / jnp.expm1(2.0 * rate)
    gain = -jnp.expm1(rate) * jnp.sqrt(-jnp.expm1(2.0 * rate))
    coef = jnp.broadcast_to(jnp.stack([rate, gain, tall])[:, :, None], (3, lev, cy))
    size_x, size_y = lax.axis_size("gx"), lax.axis_size("gy")
    part = lev // size_x
    tile = 8
    steps = lev // tile
    pieces = tile // part

    def levels_first(*shape):
        return pl.BlockSpec((tile,) + shape, lambda i: (i, 0, 0))

    def levels_second(*shape):
        first, *rest = shape
        return pl.BlockSpec((first, tile) + tuple(rest), lambda i: (0, i) + (0,) * len(rest))

    def whole(array):
        return pl.BlockSpec(
            array.shape, lambda i: (0,) * array.ndim, pipeline_mode=pl.Buffered(1)
        )

    params = pltpu.CompilerParams(
        dimension_semantics=("arbitrary",), vmem_limit_bytes=32 * 1024 * 1024
    )
    rows = fields * cx
    vmem = pl.BlockSpec(memory_space=pltpu.VMEM)
    local, state_x, turned_u, turned_v, wind_edge, wind_strip = pl.pallas_call(
        functools.partial(fields_kernel, members, most),
        grid=(steps,),
        in_specs=[
            pl.BlockSpec(memory_space=pltpu.SMEM),
            vmem,
            levels_second(members, cx, cy),
            levels_second(3, cy),
            levels_first(cx, cy),
            levels_first(cx, cy),
        ],
        out_specs=[
            vmem,
            pl.BlockSpec((pieces, 2 * fields, part, cy), lambda i: (i, 0, 0, 0)),
            levels_second(cx, cy),
            levels_second(cx, cy),
            pl.BlockSpec((2, 2, HALO, tile, cy), lambda i: (0, 0, 0, i, 0)),
            pl.BlockSpec((2, cx, tile, cy), lambda i: (0, 0, 0, 0)),
        ],
        out_shape=[
            pltpu.VMEM((lev * rows, cy), jnp.float32),
            pltpu.VMEM((size_x, 2 * fields, part, cy), jnp.bfloat16),
            pltpu.VMEM((cx, lev, cy), jnp.bfloat16),
            pltpu.VMEM((cx, lev, cy), jnp.bfloat16),
            pltpu.VMEM((2, 2, HALO, lev, cy), jnp.bfloat16),
            pltpu.VMEM((2, cx, tile, cy), jnp.bfloat16),
        ],
        scratch_shapes=[
            pltpu.VMEM((cx * lev, cy), jnp.float32),
            pltpu.VMEM((members * tile * cx, cy), jnp.float32),
            pltpu.VMEM((rows, tile, cy), jnp.float32),
            pltpu.VMEM((cx * tile, cy), jnp.float32),
            pltpu.VMEM((2, cx * tile, cy), jnp.float32),
        ],
        compiler_params=params,
        name="fields",
    )(note, got, ensemble, coef, wind_u, wind_v)
    local = local.reshape(lev, rows, cy)

    split_coef = jnp.moveaxis(coef.reshape(3, size_x, part, cy), 1, 0)
    swept = pl.pallas_call(
        functools.partial(carry_x_kernel, cx),
        out_shape=pltpu.VMEM((2 * fields, lev, cy), jnp.float32),
        in_specs=[vmem, vmem],
        out_specs=vmem,
        scratch_shapes=[pltpu.VMEM(state_x.shape, jnp.bfloat16)] * 3
        + [pltpu.SemaphoreType.DMA((4, size_x))],
        compiler_params=pltpu.CompilerParams(
            collective_id=1, has_side_effects=True, vmem_limit_bytes=12 * 1024 * 1024
        ),
        name="carry_x",
    )(state_x, split_coef)

    z, state_y = pl.pallas_call(
        functools.partial(rows_kernel, fields),
        grid=(steps,),
        in_specs=[vmem, levels_second(2 * fields, cy), levels_second(3, cy)],
        out_specs=[vmem, levels_second(2, rows)],
        out_shape=[
            pltpu.VMEM((lev, rows, cy), jnp.float32),
            pltpu.VMEM((2, lev, rows), jnp.bfloat16),
        ],
        scratch_shapes=[
            pltpu.VMEM((2, tile, rows), jnp.float32),
            pltpu.VMEM((cy, cy), jnp.float32),
            pltpu.VMEM((cy, cy), jnp.float32),
        ],
        compiler_params=params,
        name="rows",
    )(local, swept, coef)

    entered, wind_rows, wind_strips = pl.pallas_call(
        functools.partial(carry_y_kernel, cy),
        out_shape=[pltpu.VMEM((2, lev, rows), jnp.float32)]
        + edge_shapes(2, lev, cx, cy),
        in_specs=[vmem] * 4,
        out_specs=[vmem] * 3,
        scratch_shapes=[
            pltpu.VMEM((size_y, 2, lev, rows), jnp.bfloat16),
            pltpu.SemaphoreType.DMA((2, size_y)),
            pltpu.SemaphoreType.DMA((2, 2, 8)),
        ],
        compiler_params=pltpu.CompilerParams(
            collective_id=2, has_side_effects=True, vmem_limit_bytes=12 * 1024 * 1024
        ),
        name="carry_y",
    )(state_y, coef, wind_edge, wind_strip)

    grad_alpha, static, edge, strip = pl.pallas_call(
        functools.partial(final_kernel, members),
        grid=(steps,),
        in_specs=[vmem, levels_second(2, rows), levels_second(3, cy)],
        out_specs=[
            levels_second(members, cx, cy),
            levels_second(cx, cy),
            pl.BlockSpec((2, 1, HALO, tile, cy), lambda i: (0, 0, 0, i, 0)),
            pl.BlockSpec((1, cx, tile, cy), lambda i: (0, 0, 0, 0)),
        ],
        out_shape=[
            jax.ShapeDtypeStruct((members, lev, cx, cy), jnp.float32),
            pltpu.VMEM((cx, lev, cy), jnp.float32),
            pltpu.VMEM((2, 1, HALO, lev, cy), jnp.bfloat16),
            pltpu.VMEM((1, cx, tile, cy), jnp.bfloat16),
        ],
        scratch_shapes=[
            pltpu.VMEM((tile, cx, cy), jnp.float32),
            pltpu.VMEM((cx * tile, cy), jnp.float32),
            pltpu.VMEM((1, cx * tile, cy), jnp.float32),
        ],
        compiler_params=params,
        name="final",
    )(z, entered, coef)

    edge_rows, edge_strips = pl.pallas_call(
        halo_kernel,
        out_shape=edge_shapes(1, lev, cx, cy),
        in_specs=[vmem] * 2,
        out_specs=[vmem] * 2,
        scratch_shapes=[pltpu.SemaphoreType.DMA((2, 2, 8))],
        compiler_params=pltpu.CompilerParams(
            collective_id=5, has_side_effects=True, vmem_limit_bytes=12 * 1024 * 1024
        ),
        name="halo",
    )(edge, strip)

    def rows_of(array):
        return pl.BlockSpec(array.shape[:3] + (tile, cy), lambda i: (0, 0, 0, i, 0))

    extent = cx + 2 * HALO
    static = pl.pallas_call(
        transport_kernel,
        grid=(steps,),
        in_specs=[
            levels_second(cx, cy),
            levels_second(cx, cy),
            levels_second(cx, cy),
            rows_of(edge_rows),
            whole(edge_strips),
            rows_of(wind_rows),
            whole(wind_strips),
        ],
        out_specs=pl.BlockSpec((tile * cx, cy), lambda i: (i, 0)),
        out_shape=jax.ShapeDtypeStruct((lev * cx, cy), jnp.float32),
        scratch_shapes=[
            pltpu.VMEM((3, extent, tile, cy), jnp.float32),
            pltpu.VMEM((HALO, extent, tile, cy), jnp.float32),
            pltpu.VMEM((extent, tile, cy), jnp.float32),
            pltpu.VMEM((extent, tile, cy), jnp.float32),
            pltpu.VMEM((extent, tile, cy), jnp.float32),
        ],
        compiler_params=params,
        name="transport",
    )(static, turned_u, turned_v, edge_rows, edge_strips, wind_rows, wind_strips)
    static = static.reshape(lev, cx, cy)
    return (grad_alpha, static)


def solution(mesh):
    return jax.shard_map(
        body,
        mesh=mesh,
        in_specs=(
            P(None, "gx", "gy"),
            P(None, None, "gx", "gy"),
            P(None, "gx", "gy"),
            P(None, "gx", "gy"),
            P(),
            P(("gx", "gy"), None, None),
            P(("gx", "gy"), None),
            P(("gx", "gy"), None, None),
            P(("gx", "gy")),
            P(("gx", "gy")),
            P(("gx", "gy")),
        ),
        out_specs=(P(None, None, "gx", "gy"), P(None, "gx", "gy")),
        check_vma=False,
    )
```
